128 devices in a mesh: box: 32 (over z, x, core), col: 4 (over y).
Axes of the slice: x: 4, y: 4, z: 4, core: 2. Of those that a mesh axis runs over, the one named last changes fastest.
Arguments:
- density: bfloat16 [4096, 16, 456], P('box'), may hold values from -6 to 6
- export_ids: int32 [32, 32, 4], P('box'), may hold values from -1 to 127, as said below
- list_slot: int32 [4096, 64], P('box'), may hold values from -1 to 127, as said below
- translations: bfloat16 [64, 456, 456], P('col'), may hold values from -0.046875 to 0.046875
- patch_points: int32 [256, 1024], P('box'), may hold values from 0 to 1867775, as said below
- inverses: bfloat16 [256, 1024, 1024], P('box'), may hold values from -0.1875 to 0.1875
Outputs:
- field: bfloat16 [4096, 16, 456], P('box', 'col')
- corrected: bfloat16 [4096, 16, 456], P('box', 'col')
The draws below stay inside these ranges and needn't reach their ends.
Inputs may be any that keep to these rules, and one draw needn't show every extreme that they name: export_ids[s, d, c] is one of device s's boxes (an index below 128 within s's boxes) or -1 for an empty slot; the boxes of one pair (s, d) are distinct; a device's slots from itself and from the devices just before and after it are all filled. list_slot[b, o] is -1 where box b has no translation o, else an import slot of b's device whose export entry is not -1. `patch_points`: a patch of device d's patches has distinct points within 8 consecutive boxes that begin no more than 2 boxes before d's first box and end no more than 2 boxes after its last.
All inputs are finite; a program needn't handle non-finite values.
Results may differ from the reference program's by a relative error of at most 0.0045.
Values may be sent and summed in bfloat16 or wider, within the bound.
A program may use at most 128 MiB of HBM per device.

```python
import jax
import jax.numpy as jnp
from jax import lax

POINTS = 456
COLS = 16
OPS = 64
PATCH_PTS = 1024
BOX_DEV = 128
CAPACITY = 4
PATCH_DEV = 8
RIM = 2
SPAN = 8
BOXES = 4096
SOURCES = 32
PATCHES = 256


def shared_counts(key):
    count_key = jax.random.fold_in(key, 11)
    counts = jax.random.randint(count_key, (SOURCES, SOURCES), 0, CAPACITY + 1)
    target = jnp.arange(SOURCES)[:, None]
    anchor = jnp.arange(SOURCES)[None, :]
    nearby = jnp.abs(target - anchor) <= 1
    return jnp.where(nearby, CAPACITY, counts).astype(jnp.int32)


def draw_export_ids(key, part):
    counts = shared_counts(key)
    pick_key = jax.random.fold_in(key, 12)
    sub_keys = jax.random.split(pick_key, SOURCES * SOURCES)
    chosen = jax.vmap(lambda sub_key: jax.random.permutation(sub_key, BOX_DEV)[:CAPACITY])(sub_keys)
    chosen = chosen.reshape(SOURCES, SOURCES, CAPACITY)
    filled = jnp.arange(CAPACITY)[None, None, :] < counts.T[:, :, None]
    return jnp.where(filled, chosen, -1).astype(jnp.int32)


def draw_list_slot(key, part):
    counts = shared_counts(key)
    level_key = jax.random.fold_in(key, 13)
    present_key = jax.random.fold_in(key, 14)
    choose_key = jax.random.fold_in(key, 15)
    device = jnp.arange(BOXES) // BOX_DEV
    level = jax.random.randint(level_key, (SOURCES,), 0, 4)
    present = jax.random.randint(present_key, (BOXES, OPS), 0, 4) <= level[device][:, None]
    inclusive = jnp.cumsum(counts, axis=1)
    box_inclusive = inclusive[device]
    totals = box_inclusive[:, -1]
    drawn = jax.random.randint(choose_key, (BOXES, OPS), 0, totals[:, None])
    source = jnp.sum((box_inclusive[:, None, :] <= drawn[:, :, None]).astype(jnp.int32), axis=2)
    exclusive = box_inclusive - counts[device]
    base_slot = jnp.take_along_axis(exclusive, source, axis=1)
    slot_index = source * CAPACITY + (drawn - base_slot)
    return jnp.where(present, slot_index, -1).astype(jnp.int32)


def draw_patch_points(key, part):
    start_key = jax.random.fold_in(key, 21)
    point_key = jax.random.fold_in(key, 22)
    device = jnp.arange(PATCHES) // PATCH_DEV
    within = jnp.arange(PATCHES) % PATCH_DEV
    lowest = jnp.where(device == 0, 0, -RIM)
    highest = jnp.where(device == SOURCES - 1, BOX_DEV - SPAN, BOX_DEV + RIM - SPAN)
    random_start = jax.random.randint(start_key, (PATCHES,), lowest, highest + 1)
    start_box = jnp.where(within == 0, lowest, jnp.where(within == 1, highest, random_start))
    sub_keys = jax.random.split(point_key, PATCHES)
    offsets = jax.vmap(lambda sub_key: jax.random.permutation(sub_key, SPAN * POINTS)[:PATCH_PTS])(sub_keys)
    first_point = (device * BOX_DEV + start_box) * POINTS
    return (first_point[:, None] + offsets).astype(jnp.int32)


def steps_of(own_key, shape, cuts, smallest, largest):
    def one(axis_at, shards_of):
        heights = jax.random.uniform(jax.random.fold_in(jax.random.fold_in(own_key, 6), axis_at), (shards_of,), jnp.float32, smallest / len(cuts), largest / len(cuts))
        return jnp.repeat(jnp.exp(heights), shape[axis_at] // shards_of).reshape((-1,) + (1,) * (len(shape) - axis_at - 1))

    loudness = one(*cuts[0])
    for cut in cuts[1:]:
        loudness = loudness * one(*cut)
    return loudness


def scatter_about(key, dims, width, most, cuts=(), kind=jnp.bfloat16):
    level = steps_of(key, dims, cuts, -0.22, 0.18) if cuts else 1.0
    entries = jax.random.normal(key, dims, jnp.float32) * width * level
    return jnp.minimum(jnp.maximum(entries, -most), most).astype(kind)


def setup_inputs(seed: int = 0) -> dict:
    key_of = jax.random.split(jax.random.key(seed), 7)
    return {
        "density": scatter_about(key_of[0], (BOXES, COLS, POINTS), 1.0, 6.0, ((0, 32),)),
        "export_ids": draw_export_ids(jax.random.fold_in(key_of[6], 71), 0),
        "list_slot": draw_list_slot(jax.random.fold_in(key_of[6], 71), 0),
        "translations": scatter_about(key_of[3], (OPS, POINTS, POINTS), (POINTS * OPS // 2) ** -0.5, 0.046875, ((0, 4),)),
        "patch_points": draw_patch_points(jax.random.fold_in(key_of[6], 71), 0),
        "inverses": scatter_about(key_of[5], (PATCHES, PATCH_PTS, PATCH_PTS), PATCH_PTS ** -0.5, 0.1875, ((0, 32),)),
    }


def reference(density, export_ids, list_slot, translations, patch_points, inverses):
    device = (jnp.arange(BOXES) // BOX_DEV).astype(jnp.int32)
    live_slot = list_slot >= 0
    safe_slot = jnp.maximum(list_slot, 0)
    source = (safe_slot // CAPACITY).astype(jnp.int32)
    within = (safe_slot % CAPACITY).astype(jnp.int32)
    exported = export_ids[source, device[:, None], within]
    usable = live_slot & (exported >= 0)
    peer_box = jnp.where(usable, source * BOX_DEV + exported, 0).astype(jnp.int32)

    def add_operator(totals, pieces):
        peer_col, usable_col, operator = pieces
        gathered = jnp.take(density, peer_col, axis=0).astype(jnp.float32)
        gathered = jnp.where(usable_col[:, None, None], gathered, jnp.float32(0.0))
        term = jnp.dot(gathered.reshape(BOXES * COLS, POINTS), operator.astype(jnp.float32),
                       preferred_element_type=jnp.float32)
        return totals + term.reshape(BOXES, COLS, POINTS), None

    start_sum = jnp.zeros((BOXES, COLS, POINTS), jnp.float32)
    field_sum, _ = lax.scan(add_operator, start_sum, (peer_box.T, usable.T, translations))
    field = field_sum.astype(jnp.bfloat16)

    by_column = jnp.transpose(field, (1, 0, 2)).reshape(COLS, BOXES * POINTS)
    values = jnp.take(by_column, patch_points, axis=1)
    values = jnp.transpose(values, (1, 0, 2))

    def one_patch(pieces):
        patch_values, patch_inverse = pieces
        return jnp.dot(patch_values.astype(jnp.float32), patch_inverse.astype(jnp.float32),
                       preferred_element_type=jnp.float32)

    products = lax.map(one_patch, (values, inverses)).astype(jnp.bfloat16)
    flat_products = jnp.transpose(products, (1, 0, 2)).reshape(COLS, PATCHES * PATCH_PTS)
    correction = jnp.zeros((COLS, BOXES * POINTS), jnp.float32)
    correction = correction.at[:, patch_points.reshape(-1)].add(flat_products.astype(jnp.float32))
    correction = jnp.transpose(correction.reshape(COLS, BOXES, POINTS), (1, 0, 2))
    corrected = (field.astype(jnp.float32) + correction).astype(jnp.bfloat16)
    return (field, corrected)
```

```python
import functools

import jax
import jax.numpy as jnp
from jax import lax
from jax.experimental import pallas as pl
from jax.experimental.pallas import tpu as pltpu
from jax.sharding import PartitionSpec as P

BF = jnp.bfloat16
F32 = jnp.float32
I32 = jnp.int32
RIM = 2
SPAN = 8
NT = (((1,), (1,)), ((), ()))
TN = (((0,), (0,)), ((), ()))


def dot(a, b):
    return jnp.dot(a, b, preferred_element_type=F32)


def dot_nt(a, b):
    return lax.dot_general(a, b, NT, preferred_element_type=F32)


def iota(shape, axis):
    return lax.broadcasted_iota(I32, shape, axis)


def onehot(mask):
    return jnp.where(mask, 1.0, 0.0).astype(F32)


def kernel(
    sizes,
    dens_hbm, ids_hbm, slot_hbm, trans_hbm, pts_ref, inv_hbm,
    field_ref, corr_ref,
    ids, slots, dens, traw, tpad, inv, stage, outgoing, imp, xbuf, acc, part, recv,
    fown, bhot, halo_out, halo_in, ret_out, ret_in, cacc,
    load_sem, send_sem, recv_sem, rs_send, rs_recv, halo_send, halo_recv,
):
    (ns, cap, cols, width, boxes, groups, nops, chunk, opg) = sizes
    share = cols // groups
    wide = 512
    blocks = wide // 128
    nslot = ns * cap
    me = lax.axis_index("box")
    y = lax.axis_index("col")
    right = lax.rem(me + 1, ns)
    left = lax.rem(me + ns - 1, ns)

    barrier = pltpu.get_barrier_semaphore()

    def greet_box(k, carry):
        pl.semaphore_signal(barrier, inc=1, device_id={"box": lax.rem(me + k, ns)})
        return carry

    lax.fori_loop(1, ns, greet_box, 0)
    for k in range(1, groups):
        pl.semaphore_signal(barrier, inc=1, device_id={"col": lax.rem(y + k, groups)})

    loads = [
        pltpu.make_async_copy(ids_hbm, ids, load_sem.at[0]),
        pltpu.make_async_copy(dens_hbm, dens.at[:, 0:width], load_sem.at[1]),
        pltpu.make_async_copy(
            slot_hbm.at[pl.ds(pl.multiple_of(y * nops, nops), nops)], slots, load_sem.at[2]
        ),
        pltpu.make_async_copy(trans_hbm, traw, load_sem.at[3]),
        pltpu.make_async_copy(inv_hbm, inv, load_sem.at[4]),
    ]
    for load in loads[:4]:
        load.start()

    for c in range(cols):
        dens[c, width:wide, :] = jnp.zeros((wide - width, boxes), BF)
    imp[nslot] = jnp.zeros((cols, wide), BF)

    loads[0].wait()
    rows = []
    sub = iota((8, boxes), 0)
    lane = iota((8, boxes), 1)
    for r in range(nslot // 8):
        picked = jnp.full((8, boxes), -1, I32)
        for j in range(8):
            t = r * 8 + j
            picked = jnp.where(sub == j, ids[t // ns, t % ns], picked)
        rows.append(onehot(lane == picked))
    select = jnp.concatenate(rows, axis=0).astype(BF)

    loads[1].wait()
    for c in range(cols):
        out = dot_nt(select, dens[c])
        for a in range(cap):
            for m in range(blocks):
                stage[m, pl.ds(a * cols + c, ns, stride=cap * cols)] = out[
                    a * ns : (a + 1) * ns, m * 128 : (m + 1) * 128
                ]
    for m in range(blocks):
        outgoing[:, :, m * 128 : (m + 1) * 128] = stage[m].astype(BF).reshape(nslot, cols, 128)

    pl.semaphore_wait(barrier, ns - 1 + groups - 1)

    def exchange(k):
        dst = lax.rem(me + k, ns)
        return pltpu.make_async_remote_copy(
            src_ref=outgoing.at[pl.ds(dst * cap, cap)],
            dst_ref=imp.at[pl.ds(me * cap, cap)],
            send_sem=send_sem.at[k],
            recv_sem=recv_sem.at[k],
            device_id={"box": dst},
        )

    def start_exchange(k, carry):
        exchange(k).start()
        return carry

    lax.fori_loop(1, ns, start_exchange, 0)
    own = pltpu.make_async_copy(
        outgoing.at[pl.ds(me * cap, cap)], imp.at[pl.ds(me * cap, cap)], load_sem.at[5]
    )
    own.start()
    loads[4].start()

    loads[3].wait()

    live = iota((wide, wide - 384), 1) < width - 384

    def pad_operator(o, carry):
        tpad[o, 0:width, 0:width] = traw[o]
        tpad[o, :, 384:] = jnp.where(live, tpad[o, :, 384:], 0.0)
        tpad[o, width:, :] = jnp.zeros((wide - width, wide), BF)
        return carry

    lax.fori_loop(0, nops, pad_operator, 0)

    anchor = (me * boxes - RIM) * width
    local = pts_ref[...] - anchor
    box_of = jnp.floor((local.astype(F32) + 0.5) * (1.0 / width)).astype(I32)
    inner = local - box_of * width
    first = jnp.minimum(jnp.min(box_of, axis=1, keepdims=True), boxes + 2 * RIM - SPAN)
    npatch, psize = pts_ref.shape
    high = jnp.right_shift(inner, 7) * SPAN + (box_of - first)
    low = jnp.bitwise_and(inner, 127)
    sub128 = iota((128, psize), 0)
    for p in range(npatch):
        bhot[p] = onehot(sub128 == low[p : p + 1]).astype(BF)
    firsts = jnp.broadcast_to(first, (npatch, boxes))
    window = [firsts[p : p + 1] + iota((SPAN, boxes), 0) for p in range(npatch)]
    window = jnp.concatenate(window, axis=0)
    lane64 = iota(window.shape, 1)
    pick_own = onehot(window == lane64 + RIM).astype(BF)
    pick_rim = []
    for c in range(share):
        at = jnp.right_shift(lane64, 1)
        odd = jnp.bitwise_and(lane64, 1)
        low_rim = (at == c) & (window == odd)
        high_rim = (at == c + 8) & (window == odd + boxes + RIM)
        pick_rim.append(onehot(low_rim | high_rim).astype(BF)[:, 0:32])

    slots_ready = loads[2]
    slots_ready.wait()
    own.wait()

    def wait_exchange(k, carry):
        exchange(k).wait()
        return carry

    lax.fori_loop(1, ns, wait_exchange, 0)

    nchunk = boxes // chunk

    def send_part(q, k):
        peer = lax.rem(y + k, groups)
        b0 = pl.multiple_of(q * chunk, chunk)
        return pltpu.make_async_remote_copy(
            src_ref=part.at[pl.ds(peer * share, share), pl.ds(b0, chunk)],
            dst_ref=recv.at[k - 1, :, pl.ds(b0, chunk)],
            send_sem=rs_send.at[k - 1, q],
            recv_sem=rs_recv.at[k - 1, q],
            device_id={"col": peer},
        )

    def box_chunk(q, carry):
        acc[...] = jnp.zeros(acc.shape, F32)

        def op_group(g, inner_carry):
            for o in range(opg):
                for j in range(chunk):
                    s = slots[g * opg + o, q * chunk + j]
                    s = jnp.where(s < 0, nslot, s)
                    xbuf[j * cols : (j + 1) * cols, o * wide : (o + 1) * wide] = imp[s]
            weights = tpad[pl.ds(g * opg, opg)].reshape(opg * wide, wide)
            term = dot(xbuf[...], weights)
            for m in range(blocks):
                acc[m] += term[:, m * 128 : (m + 1) * 128]
            return inner_carry

        lax.fori_loop(0, nops // opg, op_group, 0)
        b0 = pl.multiple_of(q * chunk, chunk)
        for c in range(cols):
            for m in range(blocks):
                part[c, pl.ds(b0, chunk), m * 128 : (m + 1) * 128] = acc[
                    m, pl.ds(c, chunk, stride=cols)
                ].astype(BF)
        for k in range(1, groups):
            send_part(q, k).start()
        return carry

    lax.fori_loop(0, nchunk, box_chunk, 0)
    loads[4].wait()

    def wait_part(q, carry):
        for k in range(1, groups):
            send_part(q, k).wait()
        return carry

    lax.fori_loop(0, nchunk, wait_part, 0)

    row16 = iota((16, boxes), 0)
    lane16 = iota((16, boxes), 1)
    rim_low = jnp.zeros((16, wide), F32)
    rim_high = jnp.zeros((16, wide), F32)
    for c in range(share):
        total = part[y * share + c].astype(F32)
        for k in range(groups - 1):
            total = total + recv[k, c].astype(F32)
        fown[c] = total.astype(BF)
        near = (jnp.right_shift(row16, 1) == c)
        odd = jnp.bitwise_and(row16, 1)
        rim_low += dot(onehot(near & (lane16 == odd)).astype(BF), fown[c])
        rim_high += dot(onehot(near & (lane16 == odd + boxes - RIM)).astype(BF), fown[c])
    halo_out[0] = rim_high.astype(BF)
    halo_out[1] = rim_low.astype(BF)

    def swap(source, target, which, index):
        return pltpu.make_async_remote_copy(
            src_ref=source.at[which],
            dst_ref=target.at[which],
            send_sem=halo_send.at[index, which],
            recv_sem=halo_recv.at[index, which],
            device_id={"box": right if which == 0 else left},
        )

    halos = [swap(halo_out, halo_in, w, 0) for w in range(2)]
    for h in halos:
        h.start()
    eye = onehot(iota((width, wide), 0) == iota((width, wide), 1)).astype(BF)
    for c in range(share):
        field_ref[c] = dot_nt(eye, fown[c]).astype(BF)
    for h in halos:
        h.wait()

    rim_rows = halo_in[...].reshape(32, wide)
    windows = [dot(pick_own, fown[c]) + dot(pick_rim[c], rim_rows) for c in range(share)]
    sub_high = iota((blocks * SPAN, psize), 0)
    for p in range(npatch):
        pieces = [
            windows[c][p * SPAN : (p + 1) * SPAN, m * 128 : (m + 1) * 128]
            for c in range(share)
            for m in range(blocks)
        ]
        spread = dot(jnp.concatenate(pieces, axis=0).astype(BF), bhot[p])
        mask = sub_high == high[p : p + 1]
        nrow = blocks * SPAN
        values = [
            jnp.sum(jnp.where(mask, spread[c * nrow : (c + 1) * nrow], 0.0), axis=0, keepdims=True)
            for c in range(share)
        ]
        values = jnp.concatenate(values, axis=0).astype(BF)
        product = dot(values, inv[p]).astype(BF).astype(F32)
        placed = [jnp.where(mask, product[c : c + 1], 0.0) for c in range(share)]
        back = dot_nt(jnp.concatenate(placed, axis=0).astype(BF), bhot[p])
        for c in range(share):
            for m in range(blocks):
                at = c * nrow + m * SPAN
                cacc[c, p * SPAN : (p + 1) * SPAN, m * 128 : (m + 1) * 128] = back[at : at + SPAN]

    rim_sum = jnp.zeros((32, wide), F32)
    for c in range(share):
        rim_sum += lax.dot_general(pick_rim[c], cacc[c].astype(BF), TN, preferred_element_type=F32)
    ret_out[0] = rim_sum[16:32].astype(BF)
    ret_out[1] = rim_sum[0:16].astype(BF)
    returns = [swap(ret_out, ret_in, w, 1) for w in range(2)]
    for h in returns:
        h.start()
    owned = [
        fown[c].astype(F32) + lax.dot_general(pick_own, cacc[c].astype(BF), TN, preferred_element_type=F32)
        for c in range(share)
    ]
    for h in returns:
        h.wait()
    back_rows = ret_in[...].reshape(32, wide)
    for c in range(share):
        boxrow = iota((boxes, 32), 0)
        at = iota((boxes, 32), 1)
        near = jnp.bitwise_and(jnp.right_shift(at, 1), 7) == c
        odd = jnp.bitwise_and(at, 1)
        target = jnp.where(at < 16, odd, odd + boxes - RIM)
        total = owned[c] + dot(onehot(near & (boxrow == target)).astype(BF), back_rows)
        corr_ref[c] = dot_nt(eye, total.astype(BF)).astype(BF)


def body(density, export_ids, list_slot, translations, patch_points, inverses):
    boxes, cols, width = density.shape
    groups = lax.axis_size("col")
    ns, cap = export_ids.shape[1:]
    nops = translations.shape[0]
    npatch, psize = patch_points.shape
    share = cols // groups
    wide = 512
    nslot = ns * cap
    chunk, opg = 32, 4
    sizes = (ns, cap, cols, width, boxes, groups, nops, chunk, opg)
    out = jax.ShapeDtypeStruct((share, width, boxes), BF)
    anyspace = pl.BlockSpec(memory_space=pl.ANY)
    vmem = pl.BlockSpec(memory_space=pltpu.VMEM)
    dma = pltpu.SemaphoreType.DMA
    field, corrected = pl.pallas_call(
        functools.partial(kernel, sizes),
        out_shape=(out, out),
        in_specs=[anyspace, anyspace, anyspace, anyspace, vmem, anyspace],
        out_specs=(vmem, vmem),
        scratch_shapes=[
            pltpu.SMEM((cap, ns), I32),
            pltpu.SMEM((nops, boxes), I32),
            pltpu.VMEM((cols, wide, boxes), BF),
            pltpu.VMEM((nops, width, width), BF),
            pltpu.VMEM((nops, wide, wide), BF),
            pltpu.VMEM((npatch, psize, psize), BF),
            pltpu.VMEM((wide // 128, nslot * cols, 128), F32),
            pltpu.VMEM((nslot, cols, wide), BF),
            pltpu.VMEM((nslot + 1, cols, wide), BF),
            pltpu.VMEM((chunk * cols, opg * wide), BF),
            pltpu.VMEM((wide // 128, chunk * cols, 128), F32),
            pltpu.VMEM((cols, boxes, wide), BF),
            pltpu.VMEM((groups - 1, share, boxes, wide), BF),
            pltpu.VMEM((share, boxes, wide), BF),
            pltpu.VMEM((npatch, 128, psize), BF),
            pltpu.VMEM((2, 16, wide), BF),
            pltpu.VMEM((2, 16, wide), BF),
            pltpu.VMEM((2, 16, wide), BF),
            pltpu.VMEM((2, 16, wide), BF),
            pltpu.VMEM((share, npatch * SPAN, wide), F32),
            dma((6,)),
            dma((ns,)),
            dma((ns,)),
            dma((groups - 1, boxes // chunk)),
            dma((groups - 1, boxes // chunk)),
            dma((2, 2)),
            dma((2, 2)),
        ],
        compiler_params=pltpu.CompilerParams(
            collective_id=0, has_side_effects=True, vmem_limit_bytes=66 * 1000 * 1000
        ),
    )(
        jnp.transpose(density, (1, 2, 0)),
        jnp.transpose(export_ids[0], (1, 0)),
        jnp.transpose(list_slot, (1, 0)),
        translations,
        patch_points,
        inverses,
    )
    return jnp.transpose(field, (2, 0, 1)), jnp.transpose(corrected, (2, 0, 1))


def solution(mesh):
    return jax.shard_map(
        body,
        mesh=mesh,
        in_specs=(
            P("box", None, None),
            P("box", None, None),
            P("box", None),
            P("col", None, None),
            P("box", None),
            P("box", None, None),
        ),
        out_specs=(P("box", "col", None), P("box", "col", None)),
        check_vma=False,
    )
```

```python
import functools

import jax
import jax.numpy as jnp
from jax import lax
from jax.experimental import pallas as pl
from jax.experimental.pallas import tpu as pltpu
from jax.sharding import PartitionSpec as P

BF = jnp.bfloat16
F32 = jnp.float32
I32 = jnp.int32
RIM = 2
SPAN = 8
NT = (((1,), (1,)), ((), ()))
TN = (((0,), (0,)), ((), ()))


def dot(a, b):
    return jnp.dot(a, b, preferred_element_type=F32)


def dot_nt(a, b):
    return lax.dot_general(a, b, NT, preferred_element_type=F32)


def iota(shape, axis):
    return lax.broadcasted_iota(I32, shape, axis)


def onehot(mask):
    return jnp.where(mask, 1.0, 0.0).astype(F32)


def kernel(
    sizes,
    dens_hbm, ids_hbm, slot_hbm, trans_hbm, pts_ref, inv_hbm,
    field_ref, corr_ref,
    ids, slots, dens, traw, tpad, inv, stage, outgoing, imp, xbuf, acc, part, ownp, relay, recv,
    fown, bhot, halo_out, halo_in, ret_out, ret_in, cacc,
    load_sem, send_sem, recv_sem, pass_send, pass_recv, rel_send, rel_recv, rs_send, rs_recv,
    halo_send, halo_recv,
):
    (ns, cap, cols, width, boxes, groups, nops, chunk, opg) = sizes
    share = cols // groups
    wide = 512
    blocks = wide // 128
    nslot = ns * cap
    me = lax.axis_index("box")
    y = lax.axis_index("col")
    right = lax.rem(me + 1, ns)
    left = lax.rem(me + ns - 1, ns)

    barrier = pltpu.get_barrier_semaphore()

    def greet_box(k, carry):
        pl.semaphore_signal(barrier, inc=1, device_id={"box": lax.rem(me + k, ns)})
        return carry

    lax.fori_loop(1, ns, greet_box, 0)
    for k in range(1, groups):
        pl.semaphore_signal(barrier, inc=1, device_id={"col": lax.rem(y + k, groups)})

    loads = [
        pltpu.make_async_copy(ids_hbm, ids, load_sem.at[0]),
        pltpu.make_async_copy(dens_hbm, dens.at[:, 0:width], load_sem.at[1]),
        pltpu.make_async_copy(
            slot_hbm.at[pl.ds(pl.multiple_of(y * nops, nops), nops)], slots, load_sem.at[2]
        ),
        pltpu.make_async_copy(trans_hbm, traw, load_sem.at[3]),
        pltpu.make_async_copy(inv_hbm, inv, load_sem.at[4]),
    ]
    for load in loads[:4]:
        load.start()

    for c in range(cols):
        dens[c, width:wide, :] = jnp.zeros((wide - width, boxes), BF)
    imp[nslot] = jnp.zeros((cols, wide), BF)

    loads[0].wait()
    rows = []
    sub = iota((8, boxes), 0)
    lane = iota((8, boxes), 1)
    for r in range(nslot // 8):
        picked = jnp.full((8, boxes), -1, I32)
        for j in range(8):
            t = r * 8 + j
            picked = jnp.where(sub == j, ids[t // ns, t % ns], picked)
        rows.append(onehot(lane == picked))
    select = jnp.concatenate(rows, axis=0).astype(BF)

    loads[1].wait()
    for c in range(cols):
        out = dot_nt(select, dens[c])
        for a in range(cap):
            for m in range(blocks):
                stage[m, pl.ds(a * cols + c, ns, stride=cap * cols)] = out[
                    a * ns : (a + 1) * ns, m * 128 : (m + 1) * 128
                ]
    for m in range(blocks):
        outgoing[:, :, m * 128 : (m + 1) * 128] = stage[m].astype(BF).reshape(nslot, cols, 128)

    anchor = (me * boxes - RIM) * width
    local = pts_ref[...] - anchor
    box_of = jnp.floor((local.astype(F32) + 0.5) * (1.0 / width)).astype(I32)
    inner = local - box_of * width
    first = jnp.minimum(jnp.min(box_of, axis=1, keepdims=True), boxes + 2 * RIM - SPAN)
    npatch, psize = pts_ref.shape
    high = jnp.right_shift(inner, 7) * SPAN + (box_of - first)
    low = jnp.bitwise_and(inner, 127)
    sub128 = iota((128, psize), 0)
    for p in range(npatch):
        bhot[p] = onehot(sub128 == low[p : p + 1]).astype(BF)
    firsts = jnp.broadcast_to(first, (npatch, boxes))
    window = [firsts[p : p + 1] + iota((SPAN, boxes), 0) for p in range(npatch)]
    window = jnp.concatenate(window, axis=0)
    lane64 = iota(window.shape, 1)
    pick_own = onehot(window == lane64 + RIM).astype(BF)
    pick_rim = []
    for c in range(share):
        at = jnp.right_shift(lane64, 1)
        odd = jnp.bitwise_and(lane64, 1)
        low_rim = (at == c) & (window == odd)
        high_rim = (at == c + 8) & (window == odd + boxes + RIM)
        pick_rim.append(onehot(low_rim | high_rim).astype(BF)[:, 0:32])

    pl.semaphore_wait(barrier, ns - 1 + groups - 1)

    first_cap = 2 * lax.rem(y, 2)

    def exchange(k):
        dst = lax.rem(me + k, ns)
        return pltpu.make_async_remote_copy(
            src_ref=outgoing.at[pl.ds(dst * cap + first_cap, 2)],
            dst_ref=imp.at[pl.ds(me * cap + first_cap, 2)],
            send_sem=send_sem.at[k],
            recv_sem=recv_sem.at[k],
            device_id={"box": dst},
        )

    def start_exchange(k, carry):
        exchange(k).start()
        return carry

    lax.fori_loop(1, ns, start_exchange, 0)
    own = pltpu.make_async_copy(
        outgoing.at[pl.ds(me * cap, cap)], imp.at[pl.ds(me * cap, cap)], load_sem.at[5]
    )
    own.start()
    loads[4].start()
    loads[3].wait()

    col_up = lax.rem(y + 1, groups)
    col_down = lax.rem(y + groups - 1, groups)

    def pass_on(k, way):
        at = lax.rem(me + ns - k, ns) * cap + first_cap + way
        return pltpu.make_async_remote_copy(
            src_ref=imp.at[at],
            dst_ref=imp.at[at],
            send_sem=pass_send.at[way, k],
            recv_sem=pass_recv.at[way, k],
            device_id={"col": col_down if way == 0 else col_up},
        )

    live = iota((wide, wide - 384), 1) < width - 384

    def pad_operator(o):
        tpad[o, 0:width, 0:width] = traw[o]
        tpad[o, :, 384:] = jnp.where(live, tpad[o, :, 384:], 0.0)
        tpad[o, width:, :] = jnp.zeros((wide - width, wide), BF)

    def relay_boxes(k):
        exchange(k).wait_recv()
        pass_on(k, 0).start()
        pass_on(k, 1).start()

    def relay_and_pad(o, carry):
        pad_operator(o)
        relay_boxes(2 * o + 1)
        relay_boxes(2 * o + 2)
        return carry

    lax.fori_loop(0, nops - 1, relay_and_pad, 0)
    pad_operator(nops - 1)
    relay_boxes(ns - 1)

    loads[2].wait()
    own.wait()

    def wait_exchange(k, carry):
        exchange(k).wait_send()
        pass_on(k, 0).wait()
        pass_on(k, 1).wait()
        return carry

    lax.fori_loop(1, ns, wait_exchange, 0)

    nchunk = boxes // chunk
    half = chunk // 2
    opposite = lax.rem(y + 2, groups)
    towards = (col_up, col_down)

    def turn(i):
        return lax.rem(i + nchunk - 1, nchunk)

    def send_relay(i, way):
        q = turn(i)
        return pltpu.make_async_remote_copy(
            src_ref=part.at[
                pl.ds(opposite * share, share), pl.ds(pl.multiple_of(q * chunk + way * half, half), half)
            ],
            dst_ref=relay.at[way, :, pl.ds(pl.multiple_of(q * half, half), half)],
            send_sem=rel_send.at[way, i],
            recv_sem=rel_recv.at[way, i],
            device_id={"col": towards[way]},
        )

    def send_part(i, way):
        b0 = pl.multiple_of(turn(i) * chunk, chunk)
        return pltpu.make_async_remote_copy(
            src_ref=part.at[pl.ds(towards[way] * share, share), pl.ds(b0, chunk)],
            dst_ref=recv.at[way, :, pl.ds(b0, chunk)],
            send_sem=rs_send.at[way, i],
            recv_sem=rs_recv.at[way, i],
            device_id={"col": towards[way]},
        )

    def combine(i):
        q = turn(i)
        for way in range(2):
            send_relay(i, way).wait()
            b0 = pl.multiple_of(q * chunk + way * half, half)
            r0 = pl.multiple_of(q * half, half)
            for c in range(share):
                mine = part[towards[way] * share + c, pl.ds(b0, half)].astype(F32)
                mine = mine + relay[way, c, pl.ds(r0, half)].astype(F32)
                part[towards[way] * share + c, pl.ds(b0, half)] = mine.astype(BF)
            send_part(i, way).start()

    def wait_part(i):
        for way in range(2):
            send_part(i, way).wait()

    def summed(c, b0, count):
        total = ownp[c, b0 : b0 + count]
        for way in range(2):
            total = total + recv[way, c, b0 : b0 + count].astype(F32)
        return total.astype(BF)

    def swap(source, target, which, index):
        return pltpu.make_async_remote_copy(
            src_ref=source.at[which],
            dst_ref=target.at[which],
            send_sem=halo_send.at[index, which],
            recv_sem=halo_recv.at[index, which],
            device_id={"box": right if which == 0 else left},
        )

    halos = [swap(halo_out, halo_in, w, 0) for w in range(2)]

    def send_rims():
        wait_part(0)
        wait_part(1)
        row16 = iota((16, 16), 0)
        lane16 = iota((16, 16), 1)
        odd = jnp.bitwise_and(row16, 1)
        rim_low = jnp.zeros((16, wide), F32)
        rim_high = jnp.zeros((16, wide), F32)
        for c in range(share):
            near = jnp.right_shift(row16, 1) == c
            rim_low += dot(onehot(near & (lane16 == odd)).astype(BF), summed(c, 0, 16))
            rim_high += dot(onehot(near & (lane16 == odd + 16 - RIM)).astype(BF), summed(c, boxes - 16, 16))
        halo_out[0] = rim_high.astype(BF)
        halo_out[1] = rim_low.astype(BF)
        for h in halos:
            h.start()

    def box_chunk(i, carry):
        q = turn(i)
        acc[...] = jnp.zeros(acc.shape, F32)

        def op_group(g, inner_carry):
            for o in range(opg):
                for j in range(chunk):
                    s = slots[g * opg + o, q * chunk + j]
                    s = jnp.where(s < 0, nslot, s)
                    xbuf[j * cols : (j + 1) * cols, o * wide : (o + 1) * wide] = imp[s]
            weights = tpad[pl.ds(g * opg, opg)].reshape(opg * wide, wide)
            term = dot(xbuf[...], weights)
            for m in range(blocks):
                acc[m] += term[:, m * 128 : (m + 1) * 128]
            return inner_carry

        lax.fori_loop(0, nops // opg, op_group, 0)
        b0 = pl.multiple_of(q * chunk, chunk)
        for m in range(blocks):
            span = slice(m * 128, (m + 1) * 128)
            for c in range(cols):
                part[c, pl.ds(b0, chunk), span] = acc[m, pl.ds(c, chunk, stride=cols)].astype(BF)
            for c in range(share):
                ownp[c, pl.ds(b0, chunk), span] = acc[m, pl.ds(y * share + c, chunk, stride=cols)]
        for way in range(2):
            send_relay(i, way).start()

        @pl.when(i >= 1)
        def _():
            combine(i - 1)

        @pl.when(i == nchunk - 1)
        def _():
            send_rims()

        return carry

    lax.fori_loop(0, nchunk, box_chunk, 0)
    combine(nchunk - 1)
    loads[4].wait()
    for i in range(2, nchunk):
        wait_part(i)

    for c in range(share):
        fown[c] = summed(c, 0, boxes)
    for h in halos:
        h.wait()

    rim_rows = halo_in[...].reshape(32, wide)
    windows = [dot(pick_own, fown[c]) + dot(pick_rim[c], rim_rows) for c in range(share)]
    sub_high = iota((blocks * SPAN, psize), 0)
    for p in range(npatch):
        pieces = [
            windows[c][p * SPAN : (p + 1) * SPAN, m * 128 : (m + 1) * 128]
            for c in range(share)
            for m in range(blocks)
        ]
        spread = dot(jnp.concatenate(pieces, axis=0).astype(BF), bhot[p])
        mask = sub_high == high[p : p + 1]
        nrow = blocks * SPAN
        values = [
            jnp.sum(jnp.where(mask, spread[c * nrow : (c + 1) * nrow], 0.0), axis=0, keepdims=True)
            for c in range(share)
        ]
        values = jnp.concatenate(values, axis=0).astype(BF)
        product = dot(values, inv[p]).astype(BF).astype(F32)
        placed = [jnp.where(mask, product[c : c + 1], 0.0) for c in range(share)]
        back = dot_nt(jnp.concatenate(placed, axis=0).astype(BF), bhot[p])
        for c in range(share):
            for m in range(blocks):
                at = c * nrow + m * SPAN
                cacc[c, p * SPAN : (p + 1) * SPAN, m * 128 : (m + 1) * 128] = back[at : at + SPAN]

    rim_sum = jnp.zeros((32, wide), F32)
    for c in range(share):
        rim_sum += lax.dot_general(pick_rim[c], cacc[c].astype(BF), TN, preferred_element_type=F32)
    ret_out[0] = rim_sum[16:32].astype(BF)
    ret_out[1] = rim_sum[0:16].astype(BF)
    returns = [swap(ret_out, ret_in, w, 1) for w in range(2)]
    for h in returns:
        h.start()
    eye = onehot(iota((width, wide), 0) == iota((width, wide), 1)).astype(BF)
    for c in range(share):
        field_ref[c] = dot_nt(eye, fown[c]).astype(BF)
    owned = [
        fown[c].astype(F32) + lax.dot_general(pick_own, cacc[c].astype(BF), TN, preferred_element_type=F32)
        for c in range(share)
    ]
    for h in returns:
        h.wait()
    back_rows = ret_in[...].reshape(32, wide)
    for c in range(share):
        boxrow = iota((boxes, 32), 0)
        at = iota((boxes, 32), 1)
        near = jnp.bitwise_and(jnp.right_shift(at, 1), 7) == c
        odd = jnp.bitwise_and(at, 1)
        target = jnp.where(at < 16, odd, odd + boxes - RIM)
        total = owned[c] + dot(onehot(near & (boxrow == target)).astype(BF), back_rows)
        corr_ref[c] = dot_nt(eye, total.astype(BF)).astype(BF)


def body(density, export_ids, list_slot, translations, patch_points, inverses):
    boxes, cols, width = density.shape
    groups = lax.axis_size("col")
    ns, cap = export_ids.shape[1:]
    nops = translations.shape[0]
    npatch, psize = patch_points.shape
    share = cols // groups
    wide = 512
    nslot = ns * cap
    chunk, opg = 32, 4
    sizes = (ns, cap, cols, width, boxes, groups, nops, chunk, opg)
    out = jax.ShapeDtypeStruct((share, width, boxes), BF)
    anyspace = pl.BlockSpec(memory_space=pl.ANY)
    vmem = pl.BlockSpec(memory_space=pltpu.VMEM)
    dma = pltpu.SemaphoreType.DMA
    field, corrected = pl.pallas_call(
        functools.partial(kernel, sizes),
        out_shape=(out, out),
        in_specs=[anyspace, anyspace, anyspace, anyspace, vmem, anyspace],
        out_specs=(vmem, vmem),
        scratch_shapes=[
            pltpu.SMEM((cap, ns), I32),
            pltpu.SMEM((nops, boxes), I32),
            pltpu.VMEM((cols, wide, boxes), BF),
            pltpu.VMEM((nops, width, width), BF),
            pltpu.VMEM((nops, wide, wide), BF),
            pltpu.VMEM((npatch, psize, psize), BF),
            pltpu.VMEM((wide // 128, nslot * cols, 128), F32),
            pltpu.VMEM((nslot, cols, wide), BF),
            pltpu.VMEM((nslot + 1, cols, wide), BF),
            pltpu.VMEM((chunk * cols, opg * wide), BF),
            pltpu.VMEM((wide // 128, chunk * cols, 128), F32),
            pltpu.VMEM((cols, boxes, wide), BF),
            pltpu.VMEM((share, boxes, wide), F32),
            pltpu.VMEM((2, share, boxes // 2, wide), BF),
            pltpu.VMEM((2, share, boxes, wide), BF),
            pltpu.VMEM((share, boxes, wide), BF),
            pltpu.VMEM((npatch, 128, psize), BF),
            pltpu.VMEM((2, 16, wide), BF),
            pltpu.VMEM((2, 16, wide), BF),
            pltpu.VMEM((2, 16, wide), BF),
            pltpu.VMEM((2, 16, wide), BF),
            pltpu.VMEM((share, npatch * SPAN, wide), F32),
            dma((6,)),
            dma((ns,)),
            dma((ns,)),
            dma((2, ns)),
            dma((2, ns)),
            dma((2, boxes // chunk)),
            dma((2, boxes // chunk)),
            dma((2, boxes // chunk)),
            dma((2, boxes // chunk)),
            dma((2, 2)),
            dma((2, 2)),
        ],
        compiler_params=pltpu.CompilerParams(
            collective_id=0, has_side_effects=True, vmem_limit_bytes=66 * 1000 * 1000
        ),
    )(
        jnp.transpose(density, (1, 2, 0)),
        jnp.transpose(export_ids[0], (1, 0)),
        jnp.transpose(list_slot, (1, 0)),
        translations,
        patch_points,
        inverses,
    )
    return jnp.transpose(field, (2, 0, 1)), jnp.transpose(corrected, (2, 0, 1))


def solution(mesh):
    return jax.shard_map(
        body,
        mesh=mesh,
        in_specs=(
            P("box", None, None),
            P("box", None, None),
            P("box", None),
            P("col", None, None),
            P("box", None),
            P("box", None, None),
        ),
        out_specs=(P("box", "col", None), P("box", "col", None)),
        check_vma=False,
    )
```

```python
import functools

import jax
import jax.numpy as jnp
from jax import lax
from jax.experimental import pallas as pl
from jax.experimental.pallas import tpu as pltpu
from jax.sharding import PartitionSpec as P

BF = jnp.bfloat16
F32 = jnp.float32
I32 = jnp.int32
RIM = 2
SPAN = 8
NT = (((1,), (1,)), ((), ()))
TN = (((0,), (0,)), ((), ()))


def dot(a, b):
    return jnp.dot(a, b, preferred_element_type=F32)


def dot_nt(a, b):
    return lax.dot_general(a, b, NT, preferred_element_type=F32)


def iota(shape, axis):
    return lax.broadcasted_iota(I32, shape, axis)


def onehot(mask):
    return jnp.where(mask, 1.0, 0.0).astype(F32)


def kernel(
    sizes,
    dens_hbm, ids_hbm, slot_hbm, trans_hbm, pts_ref, inv_hbm,
    field_ref, corr_ref,
    ids, slots, dens, traw, tpad, inv, stage, outgoing, imp, xbuf, acc, part, ownp, relay, recv,
    fown, bhot, halo_out, halo_in, ret_out, ret_in, cacc,
    load_sem, send_sem, recv_sem, pass_send, pass_recv, rel_send, rel_recv, rs_send, rs_recv,
    halo_send, halo_recv,
):
    (ns, cap, cols, width, boxes, groups, nops, chunk, opg) = sizes
    share = cols // groups
    wide = 512
    blocks = wide // 128
    nslot = ns * cap
    me = lax.axis_index("box")
    y = lax.axis_index("col")
    right = lax.rem(me + 1, ns)
    left = lax.rem(me + ns - 1, ns)

    barrier = pltpu.get_barrier_semaphore()

    def greet_box(k, carry):
        pl.semaphore_signal(barrier, inc=1, device_id={"box": lax.rem(me + k, ns)})
        return carry

    lax.fori_loop(1, ns, greet_box, 0)
    for k in range(1, groups):
        pl.semaphore_signal(barrier, inc=1, device_id={"col": lax.rem(y + k, groups)})

    loads = [
        pltpu.make_async_copy(ids_hbm, ids, load_sem.at[0]),
        pltpu.make_async_copy(dens_hbm, dens.at[:, 0:width], load_sem.at[1]),
        pltpu.make_async_copy(
            slot_hbm.at[pl.ds(pl.multiple_of(y * nops, nops), nops)], slots, load_sem.at[2]
        ),
        pltpu.make_async_copy(trans_hbm, traw, load_sem.at[3]),
        pltpu.make_async_copy(inv_hbm, inv, load_sem.at[4]),
    ]
    for load in loads[:4]:
        load.start()

    for c in range(cols):
        dens[c, width:wide, :] = jnp.zeros((wide - width, boxes), BF)
    imp[nslot] = jnp.zeros((cols, wide), BF)

    loads[0].wait()
    rows = []
    sub = iota((8, boxes), 0)
    lane = iota((8, boxes), 1)
    for r in range(nslot // 8):
        picked = jnp.full((8, boxes), -1, I32)
        for j in range(8):
            t = r * 8 + j
            picked = jnp.where(sub == j, ids[t // ns, t % ns], picked)
        rows.append(onehot(lane == picked))
    select = jnp.concatenate(rows, axis=0).astype(BF)

    loads[1].wait()
    for c in range(cols):
        out = dot_nt(select, dens[c])
        for a in range(cap):
            for m in range(blocks):
                stage[m, pl.ds(a * cols + c, ns, stride=cap * cols)] = out[
                    a * ns : (a + 1) * ns, m * 128 : (m + 1) * 128
                ]
    for m in range(blocks):
        outgoing[:, :, m * 128 : (m + 1) * 128] = stage[m].astype(BF).reshape(nslot, cols, 128)

    anchor = (me * boxes - RIM) * width
    local = pts_ref[...] - anchor
    box_of = jnp.floor((local.astype(F32) + 0.5) * (1.0 / width)).astype(I32)
    inner = local - box_of * width
    first = jnp.minimum(jnp.min(box_of, axis=1, keepdims=True), boxes + 2 * RIM - SPAN)
    npatch, psize = pts_ref.shape
    high = jnp.right_shift(inner, 7) * SPAN + (box_of - first)
    low = jnp.bitwise_and(inner, 127)
    sub128 = iota((128, psize), 0)
    for p in range(npatch):
        bhot[p] = onehot(sub128 == low[p : p + 1]).astype(BF)
    firsts = jnp.broadcast_to(first, (npatch, boxes))
    window = [firsts[p : p + 1] + iota((SPAN, boxes), 0) for p in range(npatch)]
    window = jnp.concatenate(window, axis=0)
    lane64 = iota(window.shape, 1)
    pick_own = onehot(window == lane64 + RIM).astype(BF)
    pick_rim = []
    for c in range(share):
        at = jnp.right_shift(lane64, 1)
        odd = jnp.bitwise_and(lane64, 1)
        low_rim = (at == c) & (window == odd)
        high_rim = (at == c + 8) & (window == odd + boxes + RIM)
        pick_rim.append(onehot(low_rim | high_rim).astype(BF)[:, 0:32])

    pl.semaphore_wait(barrier, ns - 1 + groups - 1)

    first_cap = 2 * lax.rem(y, 2)

    def shifted(k, sign):
        z = lax.rem(me // 8 + sign * (k // 8) + 4, 4)
        x = lax.rem(lax.rem(me // 2, 4) + sign * lax.rem(k // 2, 4) + 4, 4)
        core = lax.rem(lax.rem(me, 2) + lax.rem(k, 2), 2)
        return z * 8 + x * 2 + core

    def exchange(j):
        k = lax.rem(j * 11, ns)
        dst = shifted(k, 1)
        return pltpu.make_async_remote_copy(
            src_ref=outgoing.at[pl.ds(dst * cap + first_cap, 2)],
            dst_ref=imp.at[pl.ds(me * cap + first_cap, 2)],
            send_sem=send_sem.at[j],
            recv_sem=recv_sem.at[j],
            device_id={"box": dst},
        )

    def start_exchange(j, carry):
        exchange(j).start()
        return carry

    ahead = 31
    lax.fori_loop(1, 1 + ahead, start_exchange, 0)
    own = pltpu.make_async_copy(
        outgoing.at[pl.ds(me * cap, cap)], imp.at[pl.ds(me * cap, cap)], load_sem.at[5]
    )
    own.start()
    loads[4].start()
    loads[3].wait()

    col_up = lax.rem(y + 1, groups)
    col_down = lax.rem(y + groups - 1, groups)

    def pass_on(k, way):
        at = shifted(lax.rem(k * 11, ns), -1) * cap + first_cap + way
        return pltpu.make_async_remote_copy(
            src_ref=imp.at[at],
            dst_ref=imp.at[at],
            send_sem=pass_send.at[way, k],
            recv_sem=pass_recv.at[way, k],
            device_id={"col": col_down if way == 0 else col_up},
        )

    live = iota((wide, wide - 384), 1) < width - 384

    def pad_operator(o):
        tpad[o, 0:width, 0:width] = traw[o]
        tpad[o, :, 384:] = jnp.where(live, tpad[o, :, 384:], 0.0)
        tpad[o, width:, :] = jnp.zeros((wide - width, wide), BF)

    def relay_boxes(k):
        exchange(k).wait()
        pass_on(k, 0).start()
        pass_on(k, 1).start()

        @pl.when(k + ahead < ns)
        def _():
            exchange(k + ahead).start()

    def relay_and_pad(o, carry):
        pad_operator(o)
        relay_boxes(2 * o + 1)
        relay_boxes(2 * o + 2)
        return carry

    lax.fori_loop(0, nops - 1, relay_and_pad, 0)
    pad_operator(nops - 1)
    relay_boxes(ns - 1)

    loads[2].wait()
    own.wait()

    def wait_exchange(k, carry):
        pass_on(k, 0).wait()
        pass_on(k, 1).wait()
        return carry

    lax.fori_loop(1, ns, wait_exchange, 0)

    nchunk = boxes // chunk
    half = chunk // 2
    opposite = lax.rem(y + 2, groups)
    towards = (col_up, col_down)

    def turn(i):
        return lax.rem(i + nchunk - 1, nchunk)

    def send_relay(i, way):
        q = turn(i)
        return pltpu.make_async_remote_copy(
            src_ref=part.at[
                pl.ds(opposite * share, share), pl.ds(pl.multiple_of(q * chunk + way * half, half), half)
            ],
            dst_ref=relay.at[way, :, pl.ds(pl.multiple_of(q * half, half), half)],
            send_sem=rel_send.at[way, i],
            recv_sem=rel_recv.at[way, i],
            device_id={"col": towards[way]},
        )

    def send_part(i, way):
        b0 = pl.multiple_of(turn(i) * chunk, chunk)
        return pltpu.make_async_remote_copy(
            src_ref=part.at[pl.ds(towards[way] * share, share), pl.ds(b0, chunk)],
            dst_ref=recv.at[way, :, pl.ds(b0, chunk)],
            send_sem=rs_send.at[way, i],
            recv_sem=rs_recv.at[way, i],
            device_id={"col": towards[way]},
        )

    def combine(i):
        q = turn(i)
        for way in range(2):
            send_relay(i, way).wait()
            b0 = pl.multiple_of(q * chunk + way * half, half)
            r0 = pl.multiple_of(q * half, half)
            for c in range(share):
                mine = part[towards[way] * share + c, pl.ds(b0, half)].astype(F32)
                mine = mine + relay[way, c, pl.ds(r0, half)].astype(F32)
                part[towards[way] * share + c, pl.ds(b0, half)] = mine.astype(BF)
            send_part(i, way).start()

    def wait_part(i):
        for way in range(2):
            send_part(i, way).wait()

    def summed(c, b0, count):
        total = ownp[c, b0 : b0 + count]
        for way in range(2):
            total = total + recv[way, c, b0 : b0 + count].astype(F32)
        return total.astype(BF)

    def swap(source, target, which, index):
        return pltpu.make_async_remote_copy(
            src_ref=source.at[which],
            dst_ref=target.at[which],
            send_sem=halo_send.at[index, which],
            recv_sem=halo_recv.at[index, which],
            device_id={"box": right if which == 0 else left},
        )

    halos = [swap(halo_out, halo_in, w, 0) for w in range(2)]

    def send_rims():
        wait_part(0)
        wait_part(1)
        row16 = iota((16, 16), 0)
        lane16 = iota((16, 16), 1)
        odd = jnp.bitwise_and(row16, 1)
        rim_low = jnp.zeros((16, wide), F32)
        rim_high = jnp.zeros((16, wide), F32)
        for c in range(share):
            near = jnp.right_shift(row16, 1) == c
            rim_low += dot(onehot(near & (lane16 == odd)).astype(BF), summed(c, 0, 16))
            rim_high += dot(onehot(near & (lane16 == odd + 16 - RIM)).astype(BF), summed(c, boxes - 16, 16))
        halo_out[0] = rim_high.astype(BF)
        halo_out[1] = rim_low.astype(BF)
        for h in halos:
            h.start()

    def box_chunk(i, carry):
        q = turn(i)
        acc[...] = jnp.zeros(acc.shape, F32)

        def op_group(g, inner_carry):
            for o in range(opg):
                for j in range(chunk):
                    s = slots[g * opg + o, q * chunk + j]
                    s = jnp.where(s < 0, nslot, s)
                    xbuf[j * cols : (j + 1) * cols, o * wide : (o + 1) * wide] = imp[s]
            weights = tpad[pl.ds(g * opg, opg)].reshape(opg * wide, wide)
            term = dot(xbuf[...], weights)
            for m in range(blocks):
                acc[m] += term[:, m * 128 : (m + 1) * 128]
            return inner_carry

        lax.fori_loop(0, nops // opg, op_group, 0)
        b0 = pl.multiple_of(q * chunk, chunk)
        for m in range(blocks):
            span = slice(m * 128, (m + 1) * 128)
            for c in range(cols):
                part[c, pl.ds(b0, chunk), span] = acc[m, pl.ds(c, chunk, stride=cols)].astype(BF)
            for c in range(share):
                ownp[c, pl.ds(b0, chunk), span] = acc[m, pl.ds(y * share + c, chunk, stride=cols)]
        for way in range(2):
            send_relay(i, way).start()

        @pl.when(i >= 1)
        def _():
            combine(i - 1)

        @pl.when(i == nchunk - 1)
        def _():
            send_rims()

        return carry

    lax.fori_loop(0, nchunk, box_chunk, 0)
    combine(nchunk - 1)
    loads[4].wait()
    for i in range(2, nchunk):
        wait_part(i)

    for c in range(share):
        fown[c] = summed(c, 0, boxes)
    for h in halos:
        h.wait()

    rim_rows = halo_in[...].reshape(32, wide)
    windows = [dot(pick_own, fown[c]) + dot(pick_rim[c], rim_rows) for c in range(share)]
    sub_high = iota((blocks * SPAN, psize), 0)
    for p in range(npatch):
        pieces = [
            windows[c][p * SPAN : (p + 1) * SPAN, m * 128 : (m + 1) * 128]
            for c in range(share)
            for m in range(blocks)
        ]
        spread = dot(jnp.concatenate(pieces, axis=0).astype(BF), bhot[p])
        mask = sub_high == high[p : p + 1]
        nrow = blocks * SPAN
        values = [
            jnp.sum(jnp.where(mask, spread[c * nrow : (c + 1) * nrow], 0.0), axis=0, keepdims=True)
            for c in range(share)
        ]
        values = jnp.concatenate(values, axis=0).astype(BF)
        product = dot(values, inv[p]).astype(BF).astype(F32)
        placed = [jnp.where(mask, product[c : c + 1], 0.0) for c in range(share)]
        back = dot_nt(jnp.concatenate(placed, axis=0).astype(BF), bhot[p])
        for c in range(share):
            for m in range(blocks):
                at = c * nrow + m * SPAN
                cacc[c, p * SPAN : (p + 1) * SPAN, m * 128 : (m + 1) * 128] = back[at : at + SPAN]

    rim_sum = jnp.zeros((32, wide), F32)
    for c in range(share):
        rim_sum += lax.dot_general(pick_rim[c], cacc[c].astype(BF), TN, preferred_element_type=F32)
    ret_out[0] = rim_sum[16:32].astype(BF)
    ret_out[1] = rim_sum[0:16].astype(BF)
    returns = [swap(ret_out, ret_in, w, 1) for w in range(2)]
    for h in returns:
        h.start()
    eye = onehot(iota((width, wide), 0) == iota((width, wide), 1)).astype(BF)
    for c in range(share):
        field_ref[c] = dot_nt(eye, fown[c]).astype(BF)
    owned = [
        fown[c].astype(F32) + lax.dot_general(pick_own, cacc[c].astype(BF), TN, preferred_element_type=F32)
        for c in range(share)
    ]
    for h in returns:
        h.wait()
    back_rows = ret_in[...].reshape(32, wide)
    for c in range(share):
        boxrow = iota((boxes, 32), 0)
        at = iota((boxes, 32), 1)
        near = jnp.bitwise_and(jnp.right_shift(at, 1), 7) == c
        odd = jnp.bitwise_and(at, 1)
        target = jnp.where(at < 16, odd, odd + boxes - RIM)
        total = owned[c] + dot(onehot(near & (boxrow == target)).astype(BF), back_rows)
        corr_ref[c] = dot_nt(eye, total.astype(BF)).astype(BF)


def body(density, export_ids, list_slot, translations, patch_points, inverses):
    boxes, cols, width = density.shape
    groups = lax.axis_size("col")
    ns, cap = export_ids.shape[1:]
    nops = translations.shape[0]
    npatch, psize = patch_points.shape
    share = cols // groups
    wide = 512
    nslot = ns * cap
    chunk, opg = 32, 4
    sizes = (ns, cap, cols, width, boxes, groups, nops, chunk, opg)
    out = jax.ShapeDtypeStruct((share, width, boxes), BF)
    anyspace = pl.BlockSpec(memory_space=pl.ANY)
    vmem = pl.BlockSpec(memory_space=pltpu.VMEM)
    dma = pltpu.SemaphoreType.DMA
    field, corrected = pl.pallas_call(
        functools.partial(kernel, sizes),
        out_shape=(out, out),
        in_specs=[anyspace, anyspace, anyspace, anyspace, vmem, anyspace],
        out_specs=(vmem, vmem),
        scratch_shapes=[
            pltpu.SMEM((cap, ns), I32),
            pltpu.SMEM((nops, boxes), I32),
            pltpu.VMEM((cols, wide, boxes), BF),
            pltpu.VMEM((nops, width, width), BF),
            pltpu.VMEM((nops, wide, wide), BF),
            pltpu.VMEM((npatch, psize, psize), BF),
            pltpu.VMEM((wide // 128, nslot * cols, 128), F32),
            pltpu.VMEM((nslot, cols, wide), BF),
            pltpu.VMEM((nslot + 1, cols, wide), BF),
            pltpu.VMEM((chunk * cols, opg * wide), BF),
            pltpu.VMEM((wide // 128, chunk * cols, 128), F32),
            pltpu.VMEM((cols, boxes, wide), BF),
            pltpu.VMEM((share, boxes, wide), F32),
            pltpu.VMEM((2, share, boxes // 2, wide), BF),
            pltpu.VMEM((2, share, boxes, wide), BF),
            pltpu.VMEM((share, boxes, wide), BF),
            pltpu.VMEM((npatch, 128, psize), BF),
            pltpu.VMEM((2, 16, wide), BF),
            pltpu.VMEM((2, 16, wide), BF),
            pltpu.VMEM((2, 16, wide), BF),
            pltpu.VMEM((2, 16, wide), BF),
            pltpu.VMEM((share, npatch * SPAN, wide), F32),
            dma((6,)),
            dma((ns,)),
            dma((ns,)),
            dma((2, ns)),
            dma((2, ns)),
            dma((2, boxes // chunk)),
            dma((2, boxes // chunk)),
            dma((2, boxes // chunk)),
            dma((2, boxes // chunk)),
            dma((2, 2)),
            dma((2, 2)),
        ],
        compiler_params=pltpu.CompilerParams(
            collective_id=0, has_side_effects=True, vmem_limit_bytes=66 * 1000 * 1000
        ),
    )(
        jnp.transpose(density, (1, 2, 0)),
        jnp.transpose(export_ids[0], (1, 0)),
        jnp.transpose(list_slot, (1, 0)),
        translations,
        patch_points,
        inverses,
    )
    return jnp.transpose(field, (2, 0, 1)), jnp.transpose(corrected, (2, 0, 1))


def solution(mesh):
    return jax.shard_map(
        body,
        mesh=mesh,
        in_specs=(
            P("box", None, None),
            P("box", None, None),
            P("box", None),
            P("col", None, None),
            P("box", None),
            P("box", None, None),
        ),
        out_specs=(P("box", "col", None), P("box", "col", None)),
        check_vma=False,
    )
```

```python
import functools

import jax
import jax.numpy as jnp
from jax import lax
from jax.experimental import pallas as pl
from jax.experimental.pallas import tpu as pltpu
from jax.sharding import PartitionSpec as P

BF = jnp.bfloat16
F32 = jnp.float32
I32 = jnp.int32
RIM = 2
SPAN = 8
NT = (((1,), (1,)), ((), ()))
TN = (((0,), (0,)), ((), ()))


def dot(a, b):
    return jnp.dot(a, b, preferred_element_type=F32)


def dot_nt(a, b):
    return lax.dot_general(a, b, NT, preferred_element_type=F32)


def iota(shape, axis):
    return lax.broadcasted_iota(I32, shape, axis)


def onehot(mask):
    return jnp.where(mask, 1.0, 0.0).astype(F32)


def kernel(
    sizes,
    dens_hbm, ids_hbm, slot_hbm, trans_hbm, pts_ref, inv_hbm,
    field_ref, corr_ref,
    ids, slots, dens, traw, tpad, inv, stage, outgoing, imp0, imp1, xbuf, xbuf2, acc, part, ownp, relay, recv,
    fown, bhot, halo_out, halo_in, ret_out, ret_in, cacc,
    load_sem, send_sem, recv_sem, pass_send, pass_recv, rel_send, rel_recv, rs_send, rs_recv,
    halo_send, halo_recv,
):
    (ns, cap, cols, width, boxes, groups, nops, chunk, opg) = sizes
    share = cols // groups
    wide = 512
    blocks = wide // 128
    nslot = ns * cap
    lot = cols // 2
    me = lax.axis_index("box")
    y = lax.axis_index("col")
    right = lax.rem(me + 1, ns)
    left = lax.rem(me + ns - 1, ns)

    barrier = pltpu.get_barrier_semaphore()

    def greet_box(k, carry):
        pl.semaphore_signal(barrier, inc=1, device_id={"box": lax.rem(me + k, ns)})
        return carry

    lax.fori_loop(1, ns, greet_box, 0)
    for k in range(1, groups):
        pl.semaphore_signal(barrier, inc=1, device_id={"col": lax.rem(y + k, groups)})

    loads = [
        pltpu.make_async_copy(ids_hbm, ids, load_sem.at[0]),
        pltpu.make_async_copy(dens_hbm, dens.at[:, 0:width], load_sem.at[1]),
        pltpu.make_async_copy(
            slot_hbm.at[pl.ds(pl.multiple_of(y * nops, nops), nops)], slots, load_sem.at[2]
        ),
        pltpu.make_async_copy(trans_hbm, traw, load_sem.at[3]),
        pltpu.make_async_copy(inv_hbm, inv, load_sem.at[4]),
    ]
    for load in loads[:4]:
        load.start()

    for c in range(cols):
        dens[c, width:wide, :] = jnp.zeros((wide - width, boxes), BF)
    imps = (imp0, imp1)
    for imp in imps:
        imp[nslot] = jnp.zeros((lot, wide), BF)

    loads[0].wait()
    rows = []
    sub = iota((8, boxes), 0)
    lane = iota((8, boxes), 1)
    for r in range(nslot // 8):
        picked = jnp.full((8, boxes), -1, I32)
        for j in range(8):
            t = r * 8 + j
            picked = jnp.where(sub == j, ids[t // ns, t % ns], picked)
        rows.append(onehot(lane == picked))
    select = jnp.concatenate(rows, axis=0).astype(BF)

    loads[1].wait()
    for c in range(cols):
        out = dot_nt(select, dens[c])
        for a in range(cap):
            for m in range(blocks):
                row = (c % share // 2) * nslot * lot + a * lot + c // share * 2 + c % 2
                stage[m, pl.ds(row, ns, stride=cap * lot)] = out[
                    a * ns : (a + 1) * ns, m * 128 : (m + 1) * 128
                ]
    for m in range(blocks):
        outgoing[:, :, :, m * 128 : (m + 1) * 128] = stage[m].astype(BF).reshape(2, nslot, lot, 128)

    anchor = (me * boxes - RIM) * width
    local = pts_ref[...] - anchor
    box_of = jnp.floor((local.astype(F32) + 0.5) * (1.0 / width)).astype(I32)
    inner = local - box_of * width
    first = jnp.minimum(jnp.min(box_of, axis=1, keepdims=True), boxes + 2 * RIM - SPAN)
    npatch, psize = pts_ref.shape
    high = jnp.right_shift(inner, 7) * SPAN + (box_of - first)
    low = jnp.bitwise_and(inner, 127)
    sub128 = iota((128, psize), 0)
    for p in range(npatch):
        bhot[p] = onehot(sub128 == low[p : p + 1]).astype(BF)
    firsts = jnp.broadcast_to(first, (npatch, boxes))
    window = [firsts[p : p + 1] + iota((SPAN, boxes), 0) for p in range(npatch)]
    window = jnp.concatenate(window, axis=0)
    lane64 = iota(window.shape, 1)
    pick_own = onehot(window == lane64 + RIM).astype(BF)
    pick_rim = []
    for c in range(share):
        at = jnp.right_shift(lane64, 1)
        odd = jnp.bitwise_and(lane64, 1)
        low_rim = (at == c) & (window == odd)
        high_rim = (at == c + 8) & (window == odd + boxes + RIM)
        pick_rim.append(onehot(low_rim | high_rim).astype(BF)[:, 0:32])

    pl.semaphore_wait(barrier, ns - 1 + groups - 1)

    first_cap = 2 * lax.rem(y, 2)

    z, x, core = me // 8, lax.rem(me // 2, 4), lax.rem(me, 2)
    z_at = [lax.rem(z + d, 4) * 8 for d in range(4)]
    x_at = [lax.rem(x + d, 4) * 2 for d in range(4)]
    core_at = [core, 1 - core]

    def shifted(j, sign):
        k = j * 11 % ns
        return z_at[sign * (k // 8) % 4] + x_at[sign * (k // 2 % 4) % 4] + core_at[k % 2]

    def exchange(h, j):
        dst = shifted(j, 1)
        return pltpu.make_async_remote_copy(
            src_ref=outgoing.at[h, pl.ds(dst * cap + first_cap, 2)],
            dst_ref=imps[h].at[pl.ds(me * cap + first_cap, 2)],
            send_sem=send_sem.at[h],
            recv_sem=recv_sem.at[h, j],
            device_id={"box": dst},
        )

    for h in range(2):
        for j in range(1, ns):
            exchange(h, j).start()
    owns = [
        pltpu.make_async_copy(
            outgoing.at[h, pl.ds(me * cap, cap)], imps[h].at[pl.ds(me * cap, cap)], load_sem.at[5 + h]
        )
        for h in range(2)
    ]
    for own in owns:
        own.start()
    loads[4].start()
    loads[3].wait()

    col_up = lax.rem(y + 1, groups)
    col_down = lax.rem(y + groups - 1, groups)

    def pass_on(h, k, way):
        at = shifted(k, -1) * cap + first_cap + way
        return pltpu.make_async_remote_copy(
            src_ref=imps[h].at[at],
            dst_ref=imps[h].at[at],
            send_sem=pass_send.at[h, way],
            recv_sem=pass_recv.at[h, way],
            device_id={"col": col_down if way == 0 else col_up},
        )

    live = iota((wide, wide - 384), 1) < width - 384

    def pad_operator(o):
        tpad[o, 0:width, 0:width] = traw[o]
        tpad[o, :, 384:] = jnp.where(live, tpad[o, :, 384:], 0.0)
        tpad[o, width:, :] = jnp.zeros((wide - width, wide), BF)

    def relay_boxes(h, k):
        exchange(h, k).wait_recv()
        pass_on(h, k, 0).start()
        pass_on(h, k, 1).start()

    def pad_some(o, carry):
        pad_operator(o)
        return carry

    lax.fori_loop(0, nops // 2, pad_some, 0)
    for j in range(1, ns):
        relay_boxes(0, j)
        if j in (9, 17):
            lax.fori_loop(nops // 2 + (j - 9) // 2, nops // 2 + (j - 9) // 2 + nops // 4, pad_some, 0)

    loads[2].wait()
    for own in owns:
        own.wait()

    def wait_passed(h):
        some = imps[h].at[0 : ns - 1]
        more = imps[h].at[0 : 2 * (ns - 1)]
        for way in range(2):
            pltpu.make_async_copy(some, some, pass_send.at[h, way]).wait()
            pltpu.make_async_copy(some, some, pass_recv.at[h, way]).wait()
        pltpu.make_async_copy(more, more, send_sem.at[h]).wait()

    wait_passed(0)

    nchunk = boxes // chunk
    nstep = 2 * nchunk
    half = chunk // 2
    relays = 8
    opposite = lax.rem(y + 2, groups)
    towards = (col_up, col_down)

    def turn(i):
        return i // nchunk, lax.rem(i + nchunk - 1, nchunk)

    def place(i):
        h, q = turn(i)
        return h * nchunk + q

    def send_relay(i, way):
        q = place(i)
        return pltpu.make_async_remote_copy(
            src_ref=part.at[opposite, q, way],
            dst_ref=relay.at[way, q],
            send_sem=rel_send.at[way, i],
            recv_sem=rel_recv.at[way, i],
            device_id={"col": towards[way]},
        )

    def send_part(i, way):
        q = place(i)
        return pltpu.make_async_remote_copy(
            src_ref=part.at[towards[way], q],
            dst_ref=recv.at[way, q],
            send_sem=rs_send.at[way, i],
            recv_sem=rs_recv.at[way, i],
            device_id={"col": towards[way]},
        )

    def combine(i):
        q = place(i)
        for way in range(2):
            send_relay(i, way).wait()
            for c in range(share // 2):
                mine = part[towards[way], q, way, c].astype(F32) + relay[way, q, c].astype(F32)
                part[towards[way], q, way, c] = mine.astype(BF)
            send_part(i, way).start()

    def wait_part(i):
        for way in range(2):
            send_part(i, way).wait()

    def summed(c, q, h):
        b0 = q * chunk + h * half
        total = ownp[c, b0 : b0 + half]
        for way in range(2):
            total = total + recv[way, c // 2 * nchunk + q, h, c % 2].astype(F32)
        return total

    def swap(source, target, which, index):
        return pltpu.make_async_remote_copy(
            src_ref=source.at[which],
            dst_ref=target.at[which],
            send_sem=halo_send.at[index, which],
            recv_sem=halo_recv.at[index, which],
            device_id={"box": right if which == 0 else left},
        )

    halos = [swap(halo_out, halo_in, w, 0) for w in range(2)]

    def send_rims():
        for i in (0, 1, nchunk, nchunk + 1):
            wait_part(i)
        row16 = iota((16, half), 0)
        lane16 = iota((16, half), 1)
        odd = jnp.bitwise_and(row16, 1)
        rim_low = jnp.zeros((16, wide), F32)
        rim_high = jnp.zeros((16, wide), F32)
        for c in range(share):
            near = jnp.right_shift(row16, 1) == c
            rim_low += dot(onehot(near & (lane16 == odd)).astype(BF), summed(c, 0, 0).astype(BF))
            rim_high += dot(onehot(near & (lane16 == odd + half - RIM)).astype(BF), summed(c, nchunk - 1, 1).astype(BF))
        halo_out[0] = rim_high.astype(BF)
        halo_out[1] = rim_low.astype(BF)
        for h in halos:
            h.start()

    def gather(h, i, g, into):
        q = turn(i)[1]
        for o in range(opg):
            for j in range(chunk):
                s = slots[g * opg + o, q * chunk + j]
                s = jnp.where(s < 0, nslot, s)
                into[j * lot : (j + 1) * lot, o * wide : (o + 1) * wide] = imps[h][s]

    def weights(g):
        return tpad[g * opg : (g + 1) * opg].reshape(opg * wide, wide)

    def relay_later(i, slot):
        for step in range(-(-(ns - 1) // (2 * relays))):

            @pl.when(i == step)
            def _():
                first = (2 * step + slot) * relays + 1
                for k in range(first, min(first + relays, ns)):
                    relay_boxes(1, k)

    def box_chunk(h, i):
        q = turn(i)[1]
        gather(h, i, 1, xbuf2)
        term = dot(xbuf[...], weights(0))
        for m in range(blocks):
            acc[m] = term[:, m * 128 : (m + 1) * 128]
        if h == 0:
            relay_later(i, 0)
        gather(h, i + 1, 0, xbuf)
        term = dot(xbuf2[...], weights(1))
        for m in range(blocks):
            acc[m] += term[:, m * 128 : (m + 1) * 128]
        if h == 0:
            relay_later(i, 1)
        b0 = pl.multiple_of(q * chunk, chunk)
        at = place(i)
        for m in range(blocks):
            span = slice(m * 128, (m + 1) * 128)
            for r in range(lot):
                for b in range(2):
                    mine = acc[m, pl.ds(b * half * lot + r, half, stride=lot)]
                    part[r // 2, at, b, r % 2, :, span] = mine.astype(BF)
            for r in range(2):
                ownp[2 * h + r, pl.ds(b0, chunk), span] = acc[m, pl.ds(y * 2 + r, chunk, stride=lot)]
        for way in range(2):
            send_relay(i, way).start()

        @pl.when(i >= 1)
        def _():
            combine(i - 1)

        @pl.when(i == nstep - 1)
        def _():
            send_rims()

    def first_half(i, carry):
        box_chunk(0, i)
        return carry

    def second_half(i, carry):
        box_chunk(1, i)
        return carry

    gather(0, 0, 0, xbuf)
    lax.fori_loop(0, nchunk, first_half, 0)
    wait_passed(1)
    gather(1, nchunk, 0, xbuf)
    lax.fori_loop(nchunk, nstep, second_half, 0)
    combine(nstep - 1)
    loads[4].wait()
    for h in range(2):
        for i in range(2, nchunk):
            wait_part(h * nchunk + i)

    for c in range(share):
        pieces = [summed(c, q, h) for q in range(nchunk) for h in range(2)]
        fown[c] = jnp.concatenate(pieces, axis=0).astype(BF)
    for h in halos:
        h.wait()

    rim_rows = halo_in[...].reshape(32, wide)
    windows = [dot(pick_own, fown[c]) + dot(pick_rim[c], rim_rows) for c in range(share)]
    sub_high = iota((blocks * SPAN, psize), 0)
    for p in range(npatch):
        pieces = [
            windows[c][p * SPAN : (p + 1) * SPAN, m * 128 : (m + 1) * 128]
            for c in range(share)
            for m in range(blocks)
        ]
        spread = dot(jnp.concatenate(pieces, axis=0).astype(BF), bhot[p])
        mask = sub_high == high[p : p + 1]
        nrow = blocks * SPAN
        values = [
            jnp.sum(jnp.where(mask, spread[c * nrow : (c + 1) * nrow], 0.0), axis=0, keepdims=True)
            for c in range(share)
        ]
        values = jnp.concatenate(values, axis=0).astype(BF)
        product = dot(values, inv[p]).astype(BF).astype(F32)
        placed = [jnp.where(mask, product[c : c + 1], 0.0) for c in range(share)]
        back = dot_nt(jnp.concatenate(placed, axis=0).astype(BF), bhot[p])
        for c in range(share):
            for m in range(blocks):
                at = c * nrow + m * SPAN
                cacc[c, p * SPAN : (p + 1) * SPAN, m * 128 : (m + 1) * 128] = back[at : at + SPAN]

    rim_sum = jnp.zeros((32, wide), F32)
    for c in range(share):
        rim_sum += lax.dot_general(pick_rim[c], cacc[c].astype(BF), TN, preferred_element_type=F32)
    ret_out[0] = rim_sum[16:32].astype(BF)
    ret_out[1] = rim_sum[0:16].astype(BF)
    returns = [swap(ret_out, ret_in, w, 1) for w in range(2)]
    for h in returns:
        h.start()
    eye = onehot(iota((width, wide), 0) == iota((width, wide), 1)).astype(BF)
    for c in range(share):
        field_ref[c] = dot_nt(eye, fown[c]).astype(BF)
    owned = [
        fown[c].astype(F32) + lax.dot_general(pick_own, cacc[c].astype(BF), TN, preferred_element_type=F32)
        for c in range(share)
    ]
    for h in returns:
        h.wait()
    back_rows = ret_in[...].reshape(32, wide)
    for c in range(share):
        boxrow = iota((boxes, 32), 0)
        at = iota((boxes, 32), 1)
        near = jnp.bitwise_and(jnp.right_shift(at, 1), 7) == c
        odd = jnp.bitwise_and(at, 1)
        target = jnp.where(at < 16, odd, odd + boxes - RIM)
        total = owned[c] + dot(onehot(near & (boxrow == target)).astype(BF), back_rows)
        corr_ref[c] = dot_nt(eye, total.astype(BF)).astype(BF)


def body(density, export_ids, list_slot, translations, patch_points, inverses):
    boxes, cols, width = density.shape
    groups = lax.axis_size("col")
    ns, cap = export_ids.shape[1:]
    nops = translations.shape[0]
    npatch, psize = patch_points.shape
    share = cols // groups
    wide = 512
    nslot = ns * cap
    chunk, opg = 32, 8
    nchunk = boxes // chunk
    sizes = (ns, cap, cols, width, boxes, groups, nops, chunk, opg)
    out = jax.ShapeDtypeStruct((share, width, boxes), BF)
    anyspace = pl.BlockSpec(memory_space=pl.ANY)
    vmem = pl.BlockSpec(memory_space=pltpu.VMEM)
    dma = pltpu.SemaphoreType.DMA
    field, corrected = pl.pallas_call(
        functools.partial(kernel, sizes),
        out_shape=(out, out),
        in_specs=[anyspace, anyspace, anyspace, anyspace, vmem, anyspace],
        out_specs=(vmem, vmem),
        scratch_shapes=[
            pltpu.SMEM((cap, ns), I32),
            pltpu.SMEM((nops, boxes), I32),
            pltpu.VMEM((cols, wide, boxes), BF),
            pltpu.VMEM((nops, width, width), BF),
            pltpu.VMEM((nops, wide, wide), BF),
            pltpu.VMEM((npatch, psize, psize), BF),
            pltpu.VMEM((wide // 128, nslot * cols, 128), F32),
            pltpu.VMEM((2, nslot, cols // 2, wide), BF),
            pltpu.VMEM((nslot + 1, cols // 2, wide), BF),
            pltpu.VMEM((nslot + 1, cols // 2, wide), BF),
            pltpu.VMEM((chunk * cols // 2, opg * wide), BF),
            pltpu.VMEM((chunk * cols // 2, opg * wide), BF),
            pltpu.VMEM((wide // 128, chunk * cols // 2, 128), F32),
            pltpu.VMEM((groups, 2 * nchunk, 2, share // 2, chunk // 2, wide), BF),
            pltpu.VMEM((share, boxes, wide), F32),
            pltpu.VMEM((2, 2 * nchunk, share // 2, chunk // 2, wide), BF),
            pltpu.VMEM((2, 2 * nchunk, 2, share // 2, chunk // 2, wide), BF),
            pltpu.VMEM((share, boxes, wide), BF),
            pltpu.VMEM((npatch, 128, psize), BF),
            pltpu.VMEM((2, 16, wide), BF),
            pltpu.VMEM((2, 16, wide), BF),
            pltpu.VMEM((2, 16, wide), BF),
            pltpu.VMEM((2, 16, wide), BF),
            pltpu.VMEM((share, npatch * SPAN, wide), F32),
            dma((7,)),
            dma((2,)),
            dma((2, ns)),
            dma((2, 2)),
            dma((2, 2)),
            dma((2, 2 * nchunk)),
            dma((2, 2 * nchunk)),
            dma((2, 2 * nchunk)),
            dma((2, 2 * nchunk)),
            dma((2, 2)),
            dma((2, 2)),
        ],
        compiler_params=pltpu.CompilerParams(
            collective_id=0, has_side_effects=True, vmem_limit_bytes=66 * 1000 * 1000
        ),
    )(
        jnp.transpose(density, (1, 2, 0)),
        jnp.transpose(export_ids[0], (1, 0)),
        jnp.transpose(list_slot, (1, 0)),
        translations,
        patch_points,
        inverses,
    )
    return jnp.transpose(field, (2, 0, 1)), jnp.transpose(corrected, (2, 0, 1))


def solution(mesh):
    return jax.shard_map(
        body,
        mesh=mesh,
        in_specs=(
            P("box", None, None),
            P("box", None, None),
            P("box", None),
            P("col", None, None),
            P("box", None),
            P("box", None, None),
        ),
        out_specs=(P("box", "col", None), P("box", "col", None)),
        check_vma=False,
    )
```

```python
import functools

import jax
import jax.numpy as jnp
from jax import lax
from jax.experimental import pallas as pl
from jax.experimental.pallas import tpu as pltpu
from jax.sharding import PartitionSpec as P

BF = jnp.bfloat16
F32 = jnp.float32
I32 = jnp.int32
RIM = 2
SPAN = 8
NT = (((1,), (1,)), ((), ()))
TN = (((0,), (0,)), ((), ()))


def dot(a, b):
    return jnp.dot(a, b, preferred_element_type=F32)


def dot_nt(a, b):
    return lax.dot_general(a, b, NT, preferred_element_type=F32)


def iota(shape, axis):
    return lax.broadcasted_iota(I32, shape, axis)


def onehot(mask):
    return jnp.where(mask, 1.0, 0.0).astype(F32)


def kernel(
    sizes,
    dens_hbm, ids_hbm, slot_hbm, trans_hbm, pts_ref, inv_hbm,
    field_ref, corr_ref,
    ids, slots, dens, traw, tpad, inv, stage, outgoing, imp0, imp1, xbuf, xbuf2, acc, part, ownp, relay, recv,
    fown, bhot, halo_out, halo_in, ret_out, ret_in, cacc,
    load_sem, send_sem, recv_sem, pass_send, pass_recv, rel_send, rel_recv, rs_send, rs_recv,
    halo_send, halo_recv,
):
    (ns, cap, cols, width, boxes, groups, nops, chunk, opg) = sizes
    share = cols // groups
    wide = 512
    blocks = wide // 128
    nslot = ns * cap
    lot = cols // 2
    me = lax.axis_index("box")
    y = lax.axis_index("col")
    right = lax.rem(me + 1, ns)
    left = lax.rem(me + ns - 1, ns)

    barrier = pltpu.get_barrier_semaphore()

    def greet_box(k, carry):
        pl.semaphore_signal(barrier, inc=1, device_id={"box": lax.rem(me + k, ns)})
        return carry

    lax.fori_loop(1, ns, greet_box, 0)
    for k in range(1, groups):
        pl.semaphore_signal(barrier, inc=1, device_id={"col": lax.rem(y + k, groups)})

    loads = [
        pltpu.make_async_copy(ids_hbm, ids, load_sem.at[0]),
        pltpu.make_async_copy(dens_hbm, dens.at[:, 0:width], load_sem.at[1]),
        pltpu.make_async_copy(
            slot_hbm.at[pl.ds(pl.multiple_of(y * nops, nops), nops)], slots, load_sem.at[2]
        ),
        pltpu.make_async_copy(trans_hbm, traw, load_sem.at[3]),
        pltpu.make_async_copy(inv_hbm, inv, load_sem.at[4]),
    ]
    for load in loads[:4]:
        load.start()

    for c in range(cols):
        dens[c, width:wide, :] = jnp.zeros((wide - width, boxes), BF)
    imps = (imp0, imp1)
    for imp in imps:
        imp[nslot] = jnp.zeros((lot, wide), BF)

    loads[0].wait()
    rows = []
    sub = iota((8, boxes), 0)
    lane = iota((8, boxes), 1)
    for r in range(nslot // 8):
        picked = jnp.full((8, boxes), -1, I32)
        for j in range(8):
            t = r * 8 + j
            picked = jnp.where(sub == j, ids[t // ns, t % ns], picked)
        rows.append(onehot(lane == picked))
    select = jnp.concatenate(rows, axis=0).astype(BF)

    loads[1].wait()
    for c in range(cols):
        out = dot_nt(select, dens[c])
        for a in range(cap):
            for m in range(blocks):
                row = (c % share // 2) * nslot * lot + a * lot + c // share * 2 + c % 2
                stage[m, pl.ds(row, ns, stride=cap * lot)] = out[
                    a * ns : (a + 1) * ns, m * 128 : (m + 1) * 128
                ]
    for m in range(blocks):
        outgoing[:, :, :, m * 128 : (m + 1) * 128] = stage[m].astype(BF).reshape(2, nslot, lot, 128)

    pl.semaphore_wait(barrier, ns - 1 + groups - 1)

    first_cap = 2 * lax.rem(y, 2)

    z, x, core = me // 8, lax.rem(me // 2, 4), lax.rem(me, 2)
    z_at = [lax.rem(z + d, 4) * 8 for d in range(4)]
    x_at = [lax.rem(x + d, 4) * 2 for d in range(4)]
    core_at = [core, 1 - core]

    def shifted(j, sign):
        k = j * 11 % ns
        return z_at[sign * (k // 8) % 4] + x_at[sign * (k // 2 % 4) % 4] + core_at[k % 2]

    def exchange(h, j):
        dst = shifted(j, 1)
        return pltpu.make_async_remote_copy(
            src_ref=outgoing.at[h, pl.ds(dst * cap + first_cap, 2)],
            dst_ref=imps[h].at[pl.ds(me * cap + first_cap, 2)],
            send_sem=send_sem.at[h],
            recv_sem=recv_sem.at[h, j],
            device_id={"box": dst},
        )

    for h in range(2):
        for j in range(1, ns):
            exchange(h, j).start()
    owns = [
        pltpu.make_async_copy(
            outgoing.at[h, pl.ds(me * cap, cap)], imps[h].at[pl.ds(me * cap, cap)], load_sem.at[5 + h]
        )
        for h in range(2)
    ]
    for own in owns:
        own.start()
    loads[4].start()
    anchor = (me * boxes - RIM) * width
    local = pts_ref[...] - anchor
    box_of = jnp.floor((local.astype(F32) + 0.5) * (1.0 / width)).astype(I32)
    inner = local - box_of * width
    first = jnp.minimum(jnp.min(box_of, axis=1, keepdims=True), boxes + 2 * RIM - SPAN)
    npatch, psize = pts_ref.shape
    high = jnp.right_shift(inner, 7) * SPAN + (box_of - first)
    low = jnp.bitwise_and(inner, 127)
    sub128 = iota((128, psize), 0)
    for p in range(npatch):
        bhot[p] = onehot(sub128 == low[p : p + 1]).astype(BF)
    firsts = jnp.broadcast_to(first, (npatch, boxes))
    window = [firsts[p : p + 1] + iota((SPAN, boxes), 0) for p in range(npatch)]
    window = jnp.concatenate(window, axis=0)
    lane64 = iota(window.shape, 1)
    pick_own = onehot(window == lane64 + RIM).astype(BF)
    pick_rim = []
    for c in range(share):
        at = jnp.right_shift(lane64, 1)
        odd = jnp.bitwise_and(lane64, 1)
        low_rim = (at == c) & (window == odd)
        high_rim = (at == c + 8) & (window == odd + boxes + RIM)
        pick_rim.append(onehot(low_rim | high_rim).astype(BF)[:, 0:32])

    loads[3].wait()

    col_up = lax.rem(y + 1, groups)
    col_down = lax.rem(y + groups - 1, groups)

    def pass_on(h, k, way):
        at = shifted(k, -1) * cap + first_cap + way
        return pltpu.make_async_remote_copy(
            src_ref=imps[h].at[at],
            dst_ref=imps[h].at[at],
            send_sem=pass_send.at[h, way],
            recv_sem=pass_recv.at[h, way],
            device_id={"col": col_down if way == 0 else col_up},
        )

    live = iota((wide, wide - 384), 1) < width - 384

    def pad_operator(o):
        tpad[o, 0:width, 0:width] = traw[o]
        tpad[o, :, 384:] = jnp.where(live, tpad[o, :, 384:], 0.0)
        tpad[o, width:, :] = jnp.zeros((wide - width, wide), BF)

    def relay_boxes(h, k):
        exchange(h, k).wait_recv()
        pass_on(h, k, 0).start()
        pass_on(h, k, 1).start()

    def pad_some(o, carry):
        pad_operator(o)
        return carry

    lax.fori_loop(0, nops // 2, pad_some, 0)
    for j in range(1, ns):
        relay_boxes(0, j)
        if j in (9, 17):
            lax.fori_loop(nops // 2 + (j - 9) // 2, nops // 2 + (j - 9) // 2 + nops // 4, pad_some, 0)

    loads[2].wait()
    for own in owns:
        own.wait()

    def wait_passed(h):
        some = imps[h].at[0 : ns - 1]
        more = imps[h].at[0 : 2 * (ns - 1)]
        for way in range(2):
            pltpu.make_async_copy(some, some, pass_send.at[h, way]).wait()
            pltpu.make_async_copy(some, some, pass_recv.at[h, way]).wait()
        pltpu.make_async_copy(more, more, send_sem.at[h]).wait()

    wait_passed(0)

    nchunk = boxes // chunk
    nstep = 2 * nchunk
    half = chunk // 2
    relays = 8
    opposite = lax.rem(y + 2, groups)
    towards = (col_up, col_down)

    def turn(i):
        return i // nchunk, lax.rem(i + nchunk - 1, nchunk)

    def place(i):
        h, q = turn(i)
        return h * nchunk + q

    def send_relay(i, way):
        q = place(i)
        return pltpu.make_async_remote_copy(
            src_ref=part.at[opposite, q, way],
            dst_ref=relay.at[way, q],
            send_sem=rel_send.at[way, i],
            recv_sem=rel_recv.at[way, i],
            device_id={"col": towards[way]},
        )

    def send_part(i, way):
        q = place(i)
        return pltpu.make_async_remote_copy(
            src_ref=part.at[towards[way], q],
            dst_ref=recv.at[way, q],
            send_sem=rs_send.at[way, i],
            recv_sem=rs_recv.at[way, i],
            device_id={"col": towards[way]},
        )

    def combine(i):
        q = place(i)
        for way in range(2):
            send_relay(i, way).wait()
            for c in range(share // 2):
                mine = part[towards[way], q, way, c].astype(F32) + relay[way, q, c].astype(F32)
                part[towards[way], q, way, c] = mine.astype(BF)
            send_part(i, way).start()

    def wait_part(i):
        for way in range(2):
            send_part(i, way).wait()

    def summed(c, q, h):
        b0 = q * chunk + h * half
        total = ownp[c, b0 : b0 + half]
        for way in range(2):
            total = total + recv[way, c // 2 * nchunk + q, h, c % 2].astype(F32)
        return total

    def swap(source, target, which, index):
        return pltpu.make_async_remote_copy(
            src_ref=source.at[which],
            dst_ref=target.at[which],
            send_sem=halo_send.at[index, which],
            recv_sem=halo_recv.at[index, which],
            device_id={"box": right if which == 0 else left},
        )

    halos = [swap(halo_out, halo_in, w, 0) for w in range(2)]

    def send_rims():
        for i in (0, 1, nchunk, nchunk + 1):
            wait_part(i)
        row16 = iota((16, half), 0)
        lane16 = iota((16, half), 1)
        odd = jnp.bitwise_and(row16, 1)
        rim_low = jnp.zeros((16, wide), F32)
        rim_high = jnp.zeros((16, wide), F32)
        for c in range(share):
            near = jnp.right_shift(row16, 1) == c
            rim_low += dot(onehot(near & (lane16 == odd)).astype(BF), summed(c, 0, 0).astype(BF))
            rim_high += dot(onehot(near & (lane16 == odd + half - RIM)).astype(BF), summed(c, nchunk - 1, 1).astype(BF))
        halo_out[0] = rim_high.astype(BF)
        halo_out[1] = rim_low.astype(BF)
        for h in halos:
            h.start()

    def gather(h, i, g, into):
        q = turn(i)[1]
        for o in range(opg):
            for j in range(chunk):
                s = slots[g * opg + o, q * chunk + j]
                s = jnp.where(s < 0, nslot, s)
                into[j * lot : (j + 1) * lot, o * wide : (o + 1) * wide] = imps[h][s]

    def weights(g):
        return tpad[g * opg : (g + 1) * opg].reshape(opg * wide, wide)

    def relay_later(i, slot):
        for step in range(-(-(ns - 1) // (2 * relays))):

            @pl.when(i == step)
            def _():
                first = (2 * step + slot) * relays + 1
                for k in range(first, min(first + relays, ns)):
                    relay_boxes(1, k)

    def box_chunk(h, i):
        q = turn(i)[1]
        gather(h, i, 1, xbuf2)
        term = dot(xbuf[...], weights(0))
        for m in range(blocks):
            acc[m] = term[:, m * 128 : (m + 1) * 128]
        if h == 0:
            relay_later(i, 0)
        gather(h, i + 1, 0, xbuf)
        term = dot(xbuf2[...], weights(1))
        for m in range(blocks):
            acc[m] += term[:, m * 128 : (m + 1) * 128]
        if h == 0:
            relay_later(i, 1)
        b0 = pl.multiple_of(q * chunk, chunk)
        at = place(i)
        for m in range(blocks):
            span = slice(m * 128, (m + 1) * 128)
            for r in range(lot):
                for b in range(2):
                    mine = acc[m, pl.ds(b * half * lot + r, half, stride=lot)]
                    part[r // 2, at, b, r % 2, :, span] = mine.astype(BF)
            for r in range(2):
                ownp[2 * h + r, pl.ds(b0, chunk), span] = acc[m, pl.ds(y * 2 + r, chunk, stride=lot)]
        for way in range(2):
            send_relay(i, way).start()

        @pl.when(i >= 1)
        def _():
            combine(i - 1)

        @pl.when(i == nstep - 1)
        def _():
            send_rims()

    def first_half(i, carry):
        box_chunk(0, i)
        return carry

    def second_half(i, carry):
        box_chunk(1, i)
        return carry

    gather(0, 0, 0, xbuf)
    lax.fori_loop(0, nchunk, first_half, 0)
    wait_passed(1)
    gather(1, nchunk, 0, xbuf)
    lax.fori_loop(nchunk, nstep, second_half, 0)
    combine(nstep - 1)
    loads[4].wait()
    for h in range(2):
        for i in range(2, nchunk):
            wait_part(h * nchunk + i)

    for c in range(share):
        pieces = [summed(c, q, h) for q in range(nchunk) for h in range(2)]
        fown[c] = jnp.concatenate(pieces, axis=0).astype(BF)
    for h in halos:
        h.wait()

    rim_rows = halo_in[...].reshape(32, wide)
    windows = [dot(pick_own, fown[c]) + dot(pick_rim[c], rim_rows) for c in range(share)]
    sub_high = iota((blocks * SPAN, psize), 0)
    for p in range(npatch):
        pieces = [
            windows[c][p * SPAN : (p + 1) * SPAN, m * 128 : (m + 1) * 128]
            for c in range(share)
            for m in range(blocks)
        ]
        spread = dot(jnp.concatenate(pieces, axis=0).astype(BF), bhot[p])
        mask = sub_high == high[p : p + 1]
        nrow = blocks * SPAN
        values = [
            jnp.sum(jnp.where(mask, spread[c * nrow : (c + 1) * nrow], 0.0), axis=0, keepdims=True)
            for c in range(share)
        ]
        values = jnp.concatenate(values, axis=0).astype(BF)
        product = dot(values, inv[p]).astype(BF).astype(F32)
        placed = [jnp.where(mask, product[c : c + 1], 0.0) for c in range(share)]
        back = dot_nt(jnp.concatenate(placed, axis=0).astype(BF), bhot[p])
        for c in range(share):
            for m in range(blocks):
                at = c * nrow + m * SPAN
                cacc[c, p * SPAN : (p + 1) * SPAN, m * 128 : (m + 1) * 128] = back[at : at + SPAN]

    rim_sum = jnp.zeros((32, wide), F32)
    for c in range(share):
        rim_sum += lax.dot_general(pick_rim[c], cacc[c].astype(BF), TN, preferred_element_type=F32)
    ret_out[0] = rim_sum[16:32].astype(BF)
    ret_out[1] = rim_sum[0:16].astype(BF)
    returns = [swap(ret_out, ret_in, w, 1) for w in range(2)]
    for h in returns:
        h.start()
    eye = onehot(iota((width, wide), 0) == iota((width, wide), 1)).astype(BF)
    for c in range(share):
        field_ref[c] = dot_nt(eye, fown[c]).astype(BF)
    owned = [
        fown[c].astype(F32) + lax.dot_general(pick_own, cacc[c].astype(BF), TN, preferred_element_type=F32)
        for c in range(share)
    ]
    for h in returns:
        h.wait()
    back_rows = ret_in[...].reshape(32, wide)
    for c in range(share):
        boxrow = iota((boxes, 32), 0)
        at = iota((boxes, 32), 1)
        near = jnp.bitwise_and(jnp.right_shift(at, 1), 7) == c
        odd = jnp.bitwise_and(at, 1)
        target = jnp.where(at < 16, odd, odd + boxes - RIM)
        total = owned[c] + dot(onehot(near & (boxrow == target)).astype(BF), back_rows)
        corr_ref[c] = dot_nt(eye, total.astype(BF)).astype(BF)


def hand_over(field_ref, corr_ref, field_out, corr_out, sem):
    copies = [
        pltpu.make_async_copy(field_ref, field_out, sem.at[0]),
        pltpu.make_async_copy(corr_ref, corr_out, sem.at[1]),
    ]
    for copy in copies:
        copy.start()
    for copy in copies:
        copy.wait()


def body(density, export_ids, list_slot, translations, patch_points, inverses):
    boxes, cols, width = density.shape
    groups = lax.axis_size("col")
    ns, cap = export_ids.shape[1:]
    nops = translations.shape[0]
    npatch, psize = patch_points.shape
    share = cols // groups
    wide = 512
    nslot = ns * cap
    chunk, opg = 32, 8
    nchunk = boxes // chunk
    sizes = (ns, cap, cols, width, boxes, groups, nops, chunk, opg)
    out = jax.ShapeDtypeStruct((share, width, boxes), BF)
    anyspace = pl.BlockSpec(memory_space=pl.ANY)
    vmem = pl.BlockSpec(memory_space=pltpu.VMEM)
    dma = pltpu.SemaphoreType.DMA
    field, corrected = pl.pallas_call(
        functools.partial(kernel, sizes),
        out_shape=(out, out),
        in_specs=[anyspace, anyspace, anyspace, anyspace, vmem, anyspace],
        out_specs=(vmem, vmem),
        scratch_shapes=[
            pltpu.SMEM((cap, ns), I32),
            pltpu.SMEM((nops, boxes), I32),
            pltpu.VMEM((cols, wide, boxes), BF),
            pltpu.VMEM((nops, width, width), BF),
            pltpu.VMEM((nops, wide, wide), BF),
            pltpu.VMEM((npatch, psize, psize), BF),
            pltpu.VMEM((wide // 128, nslot * cols, 128), F32),
            pltpu.VMEM((2, nslot, cols // 2, wide), BF),
            pltpu.VMEM((nslot + 1, cols // 2, wide), BF),
            pltpu.VMEM((nslot + 1, cols // 2, wide), BF),
            pltpu.VMEM((chunk * cols // 2, opg * wide), BF),
            pltpu.VMEM((chunk * cols // 2, opg * wide), BF),
            pltpu.VMEM((wide // 128, chunk * cols // 2, 128), F32),
            pltpu.VMEM((groups, 2 * nchunk, 2, share // 2, chunk // 2, wide), BF),
            pltpu.VMEM((share, boxes, wide), F32),
            pltpu.VMEM((2, 2 * nchunk, share // 2, chunk // 2, wide), BF),
            pltpu.VMEM((2, 2 * nchunk, 2, share // 2, chunk // 2, wide), BF),
            pltpu.VMEM((share, boxes, wide), BF),
            pltpu.VMEM((npatch, 128, psize), BF),
            pltpu.VMEM((2, 16, wide), BF),
            pltpu.VMEM((2, 16, wide), BF),
            pltpu.VMEM((2, 16, wide), BF),
            pltpu.VMEM((2, 16, wide), BF),
            pltpu.VMEM((share, npatch * SPAN, wide), F32),
            dma((7,)),
            dma((2,)),
            dma((2, ns)),
            dma((2, 2)),
            dma((2, 2)),
            dma((2, 2 * nchunk)),
            dma((2, 2 * nchunk)),
            dma((2, 2 * nchunk)),
            dma((2, 2 * nchunk)),
            dma((2, 2)),
            dma((2, 2)),
        ],
        compiler_params=pltpu.CompilerParams(
            collective_id=0, has_side_effects=True, vmem_limit_bytes=66 * 1000 * 1000
        ),
    )(
        jnp.transpose(density, (1, 2, 0)),
        jnp.transpose(export_ids[0], (1, 0)),
        jnp.transpose(list_slot, (1, 0)),
        translations,
        patch_points,
        inverses,
    )
    field, corrected = pl.pallas_call(
        hand_over,
        out_shape=(out, out),
        in_specs=[vmem, vmem],
        out_specs=(anyspace, anyspace),
        scratch_shapes=[dma((2,))],
    )(field, corrected)
    return jnp.transpose(field, (2, 0, 1)), jnp.transpose(corrected, (2, 0, 1))


def solution(mesh):
    return jax.shard_map(
        body,
        mesh=mesh,
        in_specs=(
            P("box", None, None),
            P("box", None, None),
            P("box", None),
            P("col", None, None),
            P("box", None),
            P("box", None, None),
        ),
        out_specs=(P("box", "col", None), P("box", "col", None)),
        check_vma=False,
    )
```

```python
import functools

import jax
import jax.numpy as jnp
from jax import lax
from jax.experimental import pallas as pl
from jax.experimental.pallas import tpu as pltpu
from jax.sharding import PartitionSpec as P

BF = jnp.bfloat16
F32 = jnp.float32
I32 = jnp.int32
RIM = 2
SPAN = 8
NT = (((1,), (1,)), ((), ()))
TN = (((0,), (0,)), ((), ()))


def dot(a, b):
    return jnp.dot(a, b, preferred_element_type=F32)


def dot_nt(a, b):
    return lax.dot_general(a, b, NT, preferred_element_type=F32)


def iota(shape, axis):
    return lax.broadcasted_iota(I32, shape, axis)


def onehot(mask):
    return jnp.where(mask, 1.0, 0.0).astype(F32)


def kernel(
    sizes,
    dens_hbm, ids_hbm, slot_hbm, trans_hbm, pts_ref, inv_hbm,
    field_ref, corr_ref,
    ids, slots, dens, traw, tpad, inv, stage, outgoing, imp0, imp1, xbuf, xbuf2, acc, part, ownp, relay, recv,
    fown, bhot, halo_out, halo_in, ret_out, ret_in, cacc,
    load_sem, send_sem, recv_sem, pass_send, pass_recv, rel_send, rel_recv, rs_send, rs_recv,
    halo_send, halo_recv,
):
    (ns, cap, cols, width, boxes, groups, nops, chunk, opg) = sizes
    share = cols // groups
    wide = 512
    blocks = wide // 128
    nslot = ns * cap
    lot = cols // 2
    me = lax.axis_index("box")
    y = lax.axis_index("col")
    right = lax.rem(me + 1, ns)
    left = lax.rem(me + ns - 1, ns)

    barrier = pltpu.get_barrier_semaphore()

    def greet_box(k, carry):
        pl.semaphore_signal(barrier, inc=1, device_id={"box": lax.rem(me + k, ns)})
        return carry

    lax.fori_loop(1, ns, greet_box, 0)
    for k in range(1, groups):
        pl.semaphore_signal(barrier, inc=1, device_id={"col": lax.rem(y + k, groups)})

    loads = [
        pltpu.make_async_copy(ids_hbm, ids, load_sem.at[0]),
        pltpu.make_async_copy(dens_hbm, dens.at[:, 0:width], load_sem.at[1]),
        pltpu.make_async_copy(
            slot_hbm.at[pl.ds(pl.multiple_of(y * nops, nops), nops)], slots, load_sem.at[2]
        ),
        pltpu.make_async_copy(trans_hbm, traw, load_sem.at[3]),
        pltpu.make_async_copy(inv_hbm, inv, load_sem.at[4]),
    ]
    for load in loads[:4]:
        load.start()

    for c in range(cols):
        dens[c, width:wide, :] = jnp.zeros((wide - width, boxes), BF)
    imps = (imp0, imp1)
    for imp in imps:
        imp[nslot] = jnp.zeros((lot, wide), BF)

    loads[0].wait()
    rows = []
    sub = iota((8, boxes), 0)
    lane = iota((8, boxes), 1)
    for r in range(nslot // 8):
        picked = jnp.full((8, boxes), -1, I32)
        for j in range(8):
            t = r * 8 + j
            picked = jnp.where(sub == j, ids[t // ns, t % ns], picked)
        rows.append(onehot(lane == picked))
    select = jnp.concatenate(rows, axis=0).astype(BF)

    loads[1].wait()
    for c in range(cols):
        out = dot_nt(select, dens[c])
        for a in range(cap):
            for m in range(blocks):
                row = (c % share // 2) * nslot * lot + a * lot + c // share * 2 + c % 2
                stage[m, pl.ds(row, ns, stride=cap * lot)] = out[
                    a * ns : (a + 1) * ns, m * 128 : (m + 1) * 128
                ]
    for m in range(blocks):
        outgoing[:, :, :, m * 128 : (m + 1) * 128] = stage[m].astype(BF).reshape(2, nslot, lot, 128)

    pl.semaphore_wait(barrier, ns - 1 + groups - 1)

    first_cap = 2 * lax.rem(y, 2)

    z, x, core = me // 8, lax.rem(me // 2, 4), lax.rem(me, 2)
    z_at = [lax.rem(z + d, 4) * 8 for d in range(4)]
    x_at = [lax.rem(x + d, 4) * 2 for d in range(4)]
    core_at = [core, 1 - core]

    def shifted(j, sign):
        k = j * 11 % ns
        return z_at[sign * (k // 8) % 4] + x_at[sign * (k // 2 % 4) % 4] + core_at[k % 2]

    def exchange(h, j):
        dst = shifted(j, 1)
        return pltpu.make_async_remote_copy(
            src_ref=outgoing.at[h, pl.ds(dst * cap + first_cap, 2)],
            dst_ref=imps[h].at[pl.ds(me * cap + first_cap, 2)],
            send_sem=send_sem.at[h],
            recv_sem=recv_sem.at[h, j],
            device_id={"box": dst},
        )

    for h in range(2):
        for j in range(1, ns):
            exchange(h, j).start()
    owns = [
        pltpu.make_async_copy(
            outgoing.at[h, pl.ds(me * cap, cap)], imps[h].at[pl.ds(me * cap, cap)], load_sem.at[5 + h]
        )
        for h in range(2)
    ]
    for own in owns:
        own.start()
    loads[4].start()
    anchor = (me * boxes - RIM) * width
    local = pts_ref[...] - anchor
    box_of = jnp.floor((local.astype(F32) + 0.5) * (1.0 / width)).astype(I32)
    inner = local - box_of * width
    first = jnp.minimum(jnp.min(box_of, axis=1, keepdims=True), boxes + 2 * RIM - SPAN)
    npatch, psize = pts_ref.shape
    high = jnp.right_shift(inner, 7) * SPAN + (box_of - first)
    low = jnp.bitwise_and(inner, 127)
    sub128 = iota((128, psize), 0)
    for p in range(npatch):
        bhot[p] = onehot(sub128 == low[p : p + 1]).astype(BF)
    firsts = jnp.broadcast_to(first, (npatch, boxes))
    window = [firsts[p : p + 1] + iota((SPAN, boxes), 0) for p in range(npatch)]
    window = jnp.concatenate(window, axis=0)
    lane64 = iota(window.shape, 1)
    pick_own = onehot(window == lane64 + RIM).astype(BF)
    pick_rim = []
    for c in range(share):
        at = jnp.right_shift(lane64, 1)
        odd = jnp.bitwise_and(lane64, 1)
        low_rim = (at == c) & (window == odd)
        high_rim = (at == c + 8) & (window == odd + boxes + RIM)
        pick_rim.append(onehot(low_rim | high_rim).astype(BF)[:, 0:32])

    loads[3].wait()

    col_up = lax.rem(y + 1, groups)
    col_down = lax.rem(y + groups - 1, groups)

    def pass_on(h, k, way):
        at = shifted(k, -1) * cap + first_cap + way
        return pltpu.make_async_remote_copy(
            src_ref=imps[h].at[at],
            dst_ref=imps[h].at[at],
            send_sem=pass_send.at[h, way],
            recv_sem=pass_recv.at[h, way],
            device_id={"col": col_down if way == 0 else col_up},
        )

    live = iota((wide, wide - 384), 1) < width - 384

    def pad_operator(o):
        tpad[o, 0:width, 0:width] = traw[o]
        tpad[o, :, 384:] = jnp.where(live, tpad[o, :, 384:], 0.0)
        tpad[o, width:, :] = jnp.zeros((wide - width, wide), BF)

    def relay_boxes(h, k):
        exchange(h, k).wait_recv()
        pass_on(h, k, 0).start()
        pass_on(h, k, 1).start()

    def pad_some(o, carry):
        pad_operator(o)
        return carry

    lax.fori_loop(0, nops // 4, pad_some, 0)
    for j in range(1, ns):
        relay_boxes(0, j)
        if j % 2 == 0 and j <= 3 * nops // 2:
            pad_operator(nops // 4 + j // 2 - 1)

    loads[2].wait()
    for own in owns:
        own.wait()

    def wait_passed(h):
        some = imps[h].at[0 : ns - 1]
        more = imps[h].at[0 : 2 * (ns - 1)]
        for way in range(2):
            pltpu.make_async_copy(some, some, pass_send.at[h, way]).wait()
            pltpu.make_async_copy(some, some, pass_recv.at[h, way]).wait()
        pltpu.make_async_copy(more, more, send_sem.at[h]).wait()

    wait_passed(0)

    nchunk = boxes // chunk
    nstep = 2 * nchunk
    half = chunk // 2
    relays = 8
    opposite = lax.rem(y + 2, groups)
    towards = (col_up, col_down)

    def turn(i):
        return i // nchunk, lax.rem(i + nchunk - 1, nchunk)

    def place(i):
        h, q = turn(i)
        return h * nchunk + q

    def send_relay(i, way):
        q = place(i)
        return pltpu.make_async_remote_copy(
            src_ref=part.at[opposite, q, way],
            dst_ref=relay.at[way, q],
            send_sem=rel_send.at[way, i],
            recv_sem=rel_recv.at[way, i],
            device_id={"col": towards[way]},
        )

    def send_part(i, way):
        q = place(i)
        return pltpu.make_async_remote_copy(
            src_ref=part.at[towards[way], q],
            dst_ref=recv.at[way, q],
            send_sem=rs_send.at[way, i],
            recv_sem=rs_recv.at[way, i],
            device_id={"col": towards[way]},
        )

    def combine(i):
        q = place(i)
        for way in range(2):
            send_relay(i, way).wait()
            for c in range(share // 2):
                mine = part[towards[way], q, way, c].astype(F32) + relay[way, q, c].astype(F32)
                part[towards[way], q, way, c] = mine.astype(BF)
            send_part(i, way).start()

    def wait_part(i):
        for way in range(2):
            send_part(i, way).wait()

    def summed(c, q, h):
        b0 = q * chunk + h * half
        total = ownp[c, b0 : b0 + half]
        for way in range(2):
            total = total + recv[way, c // 2 * nchunk + q, h, c % 2].astype(F32)
        return total

    def swap(source, target, which, index):
        return pltpu.make_async_remote_copy(
            src_ref=source.at[which],
            dst_ref=target.at[which],
            send_sem=halo_send.at[index, which],
            recv_sem=halo_recv.at[index, which],
            device_id={"box": right if which == 0 else left},
        )

    halos = [swap(halo_out, halo_in, w, 0) for w in range(2)]

    def send_rims():
        for i in (0, 1, nchunk, nchunk + 1):
            wait_part(i)
        row16 = iota((16, half), 0)
        lane16 = iota((16, half), 1)
        odd = jnp.bitwise_and(row16, 1)
        rim_low = jnp.zeros((16, wide), F32)
        rim_high = jnp.zeros((16, wide), F32)
        for c in range(share):
            near = jnp.right_shift(row16, 1) == c
            rim_low += dot(onehot(near & (lane16 == odd)).astype(BF), summed(c, 0, 0).astype(BF))
            rim_high += dot(onehot(near & (lane16 == odd + half - RIM)).astype(BF), summed(c, nchunk - 1, 1).astype(BF))
        halo_out[0] = rim_high.astype(BF)
        halo_out[1] = rim_low.astype(BF)
        for h in halos:
            h.start()

    def gather(h, i, g, into):
        q = turn(i)[1]
        for o in range(opg):
            for j in range(chunk):
                s = slots[g * opg + o, q * chunk + j]
                s = jnp.where(s < 0, nslot, s)
                into[j * lot : (j + 1) * lot, o * wide : (o + 1) * wide] = imps[h][s]

    def weights(g):
        return tpad[g * opg : (g + 1) * opg].reshape(opg * wide, wide)

    def relay_later(i, slot):
        for step in range(-(-(ns - 1) // (2 * relays))):

            @pl.when(i == step)
            def _():
                first = (2 * step + slot) * relays + 1
                for k in range(first, min(first + relays, ns)):
                    relay_boxes(1, k)

    def box_chunk(h, i):
        q = turn(i)[1]
        gather(h, i, 1, xbuf2)
        term = dot(xbuf[...], weights(0))
        for m in range(blocks):
            acc[m] = term[:, m * 128 : (m + 1) * 128]
        if h == 0:
            relay_later(i, 0)
        gather(h, i + 1, 0, xbuf)
        term = dot(xbuf2[...], weights(1))
        for m in range(blocks):
            acc[m] += term[:, m * 128 : (m + 1) * 128]
        if h == 0:
            relay_later(i, 1)
        b0 = pl.multiple_of(q * chunk, chunk)
        at = place(i)
        for m in range(blocks):
            span = slice(m * 128, (m + 1) * 128)
            for r in range(lot):
                for b in range(2):
                    mine = acc[m, pl.ds(b * half * lot + r, half, stride=lot)]
                    part[r // 2, at, b, r % 2, :, span] = mine.astype(BF)
            for r in range(2):
                ownp[2 * h + r, pl.ds(b0, chunk), span] = acc[m, pl.ds(y * 2 + r, chunk, stride=lot)]
        for way in range(2):
            send_relay(i, way).start()

        @pl.when(i >= 1)
        def _():
            combine(i - 1)

        @pl.when(i == nstep - 1)
        def _():
            send_rims()

    def first_half(i, carry):
        box_chunk(0, i)
        return carry

    def second_half(i, carry):
        box_chunk(1, i)
        return carry

    gather(0, 0, 0, xbuf)
    lax.fori_loop(0, nchunk, first_half, 0)
    wait_passed(1)
    gather(1, nchunk, 0, xbuf)
    lax.fori_loop(nchunk, nstep, second_half, 0)
    combine(nstep - 1)
    loads[4].wait()
    for h in range(2):
        for i in range(2, nchunk):
            wait_part(h * nchunk + i)

    for c in range(share):
        pieces = [summed(c, q, h) for q in range(nchunk) for h in range(2)]
        fown[c] = jnp.concatenate(pieces, axis=0).astype(BF)
    for h in halos:
        h.wait()

    rim_rows = halo_in[...].reshape(32, wide)
    windows = [dot(pick_own, fown[c]) + dot(pick_rim[c], rim_rows) for c in range(share)]
    sub_high = iota((blocks * SPAN, psize), 0)
    for p in range(npatch):
        pieces = [
            windows[c][p * SPAN : (p + 1) * SPAN, m * 128 : (m + 1) * 128]
            for c in range(share)
            for m in range(blocks)
        ]
        spread = dot(jnp.concatenate(pieces, axis=0).astype(BF), bhot[p])
        mask = sub_high == high[p : p + 1]
        nrow = blocks * SPAN
        values = [
            jnp.sum(jnp.where(mask, spread[c * nrow : (c + 1) * nrow], 0.0), axis=0, keepdims=True)
            for c in range(share)
        ]
        values = jnp.concatenate(values, axis=0).astype(BF)
        product = dot(values, inv[p]).astype(BF).astype(F32)
        placed = [jnp.where(mask, product[c : c + 1], 0.0) for c in range(share)]
        back = dot_nt(jnp.concatenate(placed, axis=0).astype(BF), bhot[p])
        for c in range(share):
            for m in range(blocks):
                at = c * nrow + m * SPAN
                cacc[c, p * SPAN : (p + 1) * SPAN, m * 128 : (m + 1) * 128] = back[at : at + SPAN]

    rim_sum = jnp.zeros((32, wide), F32)
    for c in range(share):
        rim_sum += lax.dot_general(pick_rim[c], cacc[c].astype(BF), TN, preferred_element_type=F32)
    ret_out[0] = rim_sum[16:32].astype(BF)
    ret_out[1] = rim_sum[0:16].astype(BF)
    returns = [swap(ret_out, ret_in, w, 1) for w in range(2)]
    for h in returns:
        h.start()
    eye = onehot(iota((width, wide), 0) == iota((width, wide), 1)).astype(BF)
    for c in range(share):
        field_ref[c] = dot_nt(eye, fown[c]).astype(BF)
    owned = [
        fown[c].astype(F32) + lax.dot_general(pick_own, cacc[c].astype(BF), TN, preferred_element_type=F32)
        for c in range(share)
    ]
    for h in returns:
        h.wait()
    back_rows = ret_in[...].reshape(32, wide)
    for c in range(share):
        boxrow = iota((boxes, 32), 0)
        at = iota((boxes, 32), 1)
        near = jnp.bitwise_and(jnp.right_shift(at, 1), 7) == c
        odd = jnp.bitwise_and(at, 1)
        target = jnp.where(at < 16, odd, odd + boxes - RIM)
        total = owned[c] + dot(onehot(near & (boxrow == target)).astype(BF), back_rows)
        corr_ref[c] = dot_nt(eye, total.astype(BF)).astype(BF)


def hand_over(field_ref, corr_ref, field_out, corr_out, held, load_sem, store_sem):
    share = field_ref.shape[0]
    loads, stores = [], []
    for w, (source, target) in enumerate(((field_ref, field_out), (corr_ref, corr_out))):
        for c in range(share):
            place = held.at[w, c]
            loads.append(pltpu.make_async_copy(source.at[c], place, load_sem.at[w, c]))
            stores.append(pltpu.make_async_copy(place, target.at[c], store_sem.at[w, c]))
    for load in loads:
        load.start()
    for load, store in zip(loads, stores):
        load.wait()
        store.start()
    for store in stores:
        store.wait()


def body(density, export_ids, list_slot, translations, patch_points, inverses):
    boxes, cols, width = density.shape
    groups = lax.axis_size("col")
    ns, cap = export_ids.shape[1:]
    nops = translations.shape[0]
    npatch, psize = patch_points.shape
    share = cols // groups
    wide = 512
    nslot = ns * cap
    chunk, opg = 32, 8
    nchunk = boxes // chunk
    sizes = (ns, cap, cols, width, boxes, groups, nops, chunk, opg)
    out = jax.ShapeDtypeStruct((share, width, boxes), BF)
    anyspace = pl.BlockSpec(memory_space=pl.ANY)
    vmem = pl.BlockSpec(memory_space=pltpu.VMEM)
    dma = pltpu.SemaphoreType.DMA
    field, corrected = pl.pallas_call(
        functools.partial(kernel, sizes),
        out_shape=(out, out),
        in_specs=[anyspace, anyspace, anyspace, anyspace, vmem, anyspace],
        out_specs=(vmem, vmem),
        scratch_shapes=[
            pltpu.SMEM((cap, ns), I32),
            pltpu.SMEM((nops, boxes), I32),
            pltpu.VMEM((cols, wide, boxes), BF),
            pltpu.VMEM((nops, width, width), BF),
            pltpu.VMEM((nops, wide, wide), BF),
            pltpu.VMEM((npatch, psize, psize), BF),
            pltpu.VMEM((wide // 128, nslot * cols, 128), F32),
            pltpu.VMEM((2, nslot, cols // 2, wide), BF),
            pltpu.VMEM((nslot + 1, cols // 2, wide), BF),
            pltpu.VMEM((nslot + 1, cols // 2, wide), BF),
            pltpu.VMEM((chunk * cols // 2, opg * wide), BF),
            pltpu.VMEM((chunk * cols // 2, opg * wide), BF),
            pltpu.VMEM((wide // 128, chunk * cols // 2, 128), F32),
            pltpu.VMEM((groups, 2 * nchunk, 2, share // 2, chunk // 2, wide), BF),
            pltpu.VMEM((share, boxes, wide), F32),
            pltpu.VMEM((2, 2 * nchunk, share // 2, chunk // 2, wide), BF),
            pltpu.VMEM((2, 2 * nchunk, 2, share // 2, chunk // 2, wide), BF),
            pltpu.VMEM((share, boxes, wide), BF),
            pltpu.VMEM((npatch, 128, psize), BF),
            pltpu.VMEM((2, 16, wide), BF),
            pltpu.VMEM((2, 16, wide), BF),
            pltpu.VMEM((2, 16, wide), BF),
            pltpu.VMEM((2, 16, wide), BF),
            pltpu.VMEM((share, npatch * SPAN, wide), F32),
            dma((7,)),
            dma((2,)),
            dma((2, ns)),
            dma((2, 2)),
            dma((2, 2)),
            dma((2, 2 * nchunk)),
            dma((2, 2 * nchunk)),
            dma((2, 2 * nchunk)),
            dma((2, 2 * nchunk)),
            dma((2, 2)),
            dma((2, 2)),
        ],
        compiler_params=pltpu.CompilerParams(
            collective_id=0, has_side_effects=True, vmem_limit_bytes=66 * 1000 * 1000
        ),
    )(
        jnp.transpose(density, (1, 2, 0)),
        jnp.transpose(export_ids[0], (1, 0)),
        jnp.transpose(list_slot, (1, 0)),
        translations,
        patch_points,
        inverses,
    )
    field, corrected = pl.pallas_call(
        hand_over,
        out_shape=(out, out),
        in_specs=[anyspace, anyspace],
        out_specs=(anyspace, anyspace),
        scratch_shapes=[pltpu.VMEM((2, share, width, boxes), BF), dma((2, share)), dma((2, share))],
    )(field, corrected)
    return jnp.transpose(field, (2, 0, 1)), jnp.transpose(corrected, (2, 0, 1))


def solution(mesh):
    return jax.shard_map(
        body,
        mesh=mesh,
        in_specs=(
            P("box", None, None),
            P("box", None, None),
            P("box", None),
            P("col", None, None),
            P("box", None),
            P("box", None, None),
        ),
        out_specs=(P("box", "col", None), P("box", "col", None)),
        check_vma=False,
    )
```
